32 devices in a mesh: blk: 8 (over z, core), grp: 4 (over y, x).
Axes of the slice: x: 2, y: 2, z: 4, core: 2. Of those that a mesh axis runs over, the one named last changes fastest.
Arguments:
- queries: bfloat16 [1024, 3584], P(('blk', 'grp')), may hold values from -8 to 8
- stored_documents: bfloat16 [8192, 3584], P('blk'), may hold values from -8 to 8
- positive: int32 [1024], P(('blk', 'grp')), may hold values from 0 to 8191, as said below
- last_hidden: bfloat16 [64, 3584], P(('blk', 'grp')), may hold values from -150 to 150
- norm_gain: float32 [3584], replicated, may hold values from 0.1 to 1.9
- gate_weight: bfloat16 [3584, 18944], P('grp', 'blk'), may hold values from -0.09375 to 0.09375
- up_weight: bfloat16 [3584, 18944], P('grp', 'blk'), may hold values from -0.09375 to 0.09375
- down_weight: bfloat16 [18944, 3584], P('blk', 'grp'), may hold values from -0.046875 to 0.046875
Outputs:
- losses: float32 [1024], P(('blk', 'grp'))
- passage_grads: float32 [8192, 3584], P(('blk', 'grp'))
- hidden_grads: float32 [64, 3584], P(('blk', 'grp'))
The draws below stay inside these ranges and needn't reach their ends.
Inputs may be any that keep to these rules, and one draw needn't show every extreme that they name: No two queries share a positive passage.
All inputs are finite; a program needn't handle non-finite values.
Results may differ from the reference program's by a relative error of at most 0.019.
Values may be sent and summed in bfloat16 or wider, within the bound.
A program may use at most 128 MiB of HBM per device.

```python
import math
import jax
import jax.numpy as jnp
from jax import lax

D = 3584
FF = 18944
QC = 32
PC = 1024
SUB_DEV = 2
B = 1024
NP = 8192
S = 64
N_BLK = 8
N_GRP = 4


def draw_stored_documents(key, part):
    key_entry, key_scale = jax.random.split(jax.random.fold_in(key, 13), 2)
    unit_scale = 1.0 / math.sqrt(D)
    row_index = jnp.arange(NP, dtype=jnp.float32)[:, None]
    entries = jax.random.truncated_normal(key_entry, -6.0, 6.0, (NP, D), jnp.float32)
    spread = jnp.exp(jax.random.uniform(key_scale, (NP, 1), jnp.float32, math.log(0.3), math.log(3.0)))
    rising = 0.6 + 1.2 * row_index / NP
    matrix = entries * spread * rising * unit_scale
    return matrix.astype(jnp.bfloat16)


def draw_queries(key, part):
    key_entry, key_scale = jax.random.split(jax.random.fold_in(key, 29), 2)
    unit_scale = 1.0 / math.sqrt(D)
    entries = jax.random.truncated_normal(key_entry, -6.0, 6.0, (B, D), jnp.float32)
    spread = jnp.exp(jax.random.uniform(key_scale, (B, 1), jnp.float32, math.log(0.5), math.log(1.5)))
    matrix = entries * spread * unit_scale
    return matrix.astype(jnp.bfloat16)


def draw_positive(key, part):
    shuffled = jax.random.permutation(jax.random.fold_in(key, 5), B).astype(jnp.int32)
    stride = NP // B
    return (shuffled * stride + shuffled % stride).astype(jnp.int32)


def draw_last_hidden(key, part):
    key_entry, key_rows, key_cols = jax.random.split(jax.random.fold_in(key, 41), 3)
    column_scale = jnp.exp(jax.random.uniform(key_cols, (1, D), jnp.float32, math.log(0.5), math.log(2.0)))
    entries = jax.random.truncated_normal(key_entry, -6.0, 6.0, (S, D), jnp.float32)
    row_multiplier = jnp.exp(jax.random.uniform(key_rows, (S, 1), jnp.float32, math.log(1.0), math.log(10.0)))
    matrix = entries * row_multiplier * column_scale
    return matrix.astype(jnp.bfloat16)


def block_scale(rng, shape, pieces, least, top_value):
    loudness, own = 1.0, jax.random.fold_in(rng, 6)
    for axis_at, parts in pieces:
        steps = jnp.exp(jax.random.uniform(jax.random.fold_in(own, axis_at), (parts,), jnp.float32, least / len(pieces), top_value / len(pieces)))
        loudness = loudness * jnp.repeat(steps, shape[axis_at] // parts).reshape([-1 if axis == axis_at else 1 for axis in range(len(shape))])
    return loudness


def gaussian(stream_key, dims, width, most, pieces=(), held_as=jnp.bfloat16):
    values = width * jax.random.normal(stream_key, dims, jnp.float32)
    if pieces:
        values = values * block_scale(stream_key, dims, pieces, -0.22, 0.18)
    return jnp.clip(values, -most, most).astype(held_as)


def setup_inputs(seed: int = 0) -> dict:
    keys = jax.random.split(jax.random.key(seed), 9)
    return {
        "queries": draw_queries(jax.random.fold_in(keys[8], 71), 0),
        "stored_documents": draw_stored_documents(jax.random.fold_in(keys[8], 71), 0),
        "positive": draw_positive(jax.random.fold_in(keys[8], 71), 0),
        "last_hidden": draw_last_hidden(jax.random.fold_in(keys[8], 71), 0),
        "norm_gain": jnp.clip(1.0 + 0.18 * jax.random.normal(keys[4], (D,), jnp.float32), 0.1, 1.9),
        "gate_weight": gaussian(keys[5], (D, FF), D ** -0.5, 0.09375, ((0, 4), (1, 8))),
        "up_weight": gaussian(keys[6], (D, FF), D ** -0.5, 0.09375, ((0, 4), (1, 8))),
        "down_weight": gaussian(keys[7], (FF, D), FF ** -0.5, 0.046875, ((0, 8), (1, 4))),
    }


sharpness_scale = 20.0
epsilon = 1e-06

def matmul(left_side, right_side):
    return jnp.dot(left_side.astype(jnp.float32), right_side.astype(jnp.float32), preferred_element_type=jnp.float32)

def rounded(matrix):
    return lax.optimization_barrier(matrix.astype(jnp.bfloat16)).astype(jnp.float32)

def reference(queries, stored_documents, positive, last_hidden, norm_gain, gate_weight, up_weight, down_weight):
    document_vectors_wide = stored_documents.astype(jnp.float32)
    document_subsets = document_vectors_wide.reshape(N_BLK, PC, D)
    query_lattice = queries.reshape(N_BLK, N_GRP, QC, D)
    pos_grid = positive.reshape(N_BLK, N_GRP, QC)
    column_ids = jnp.arange(NP, dtype=jnp.int32)
    passage_grads = jnp.zeros((NP, D), jnp.float32)
    loss_parts = []
    grad_parts = []
    for column in range(N_GRP):
        search_texts_across = query_lattice[:, column].reshape(N_BLK * QC, D).astype(jnp.float32)
        column_pos = pos_grid[:, column].reshape(N_BLK * QC)
        similarity_scores = sharpness_scale * jnp.dot(search_texts_across, document_vectors_wide.T, preferred_element_type=jnp.float32)
        highest = lax.optimization_barrier(jnp.max(similarity_scores, axis=1, keepdims=True))
        log_total = highest + jnp.log(lax.optimization_barrier(jnp.sum(jnp.exp(similarity_scores - highest), axis=1, keepdims=True)))
        onehot = (column_ids[None, :] == column_pos[:, None]).astype(jnp.float32)
        pos_logit = lax.optimization_barrier(jnp.sum(similarity_scores * onehot, axis=1))
        loss_parts.append((log_total[:, 0] - pos_logit).reshape(N_BLK, 1, QC))
        layer_parameters = rounded(jnp.exp(similarity_scores - log_total) - onehot)
        subset_coefficients = layer_parameters.reshape(N_BLK * QC, N_BLK, PC)
        linear_branch_ratio = sharpness_scale * jnp.einsum('zcn,cnk->czk', subset_coefficients, document_subsets)
        column_grads = lax.optimization_barrier(jnp.sum(rounded(linear_branch_ratio), axis=0))
        grad_parts.append(column_grads.reshape(N_BLK, 1, QC, D))
        document_contribution = sharpness_scale * jnp.dot(layer_parameters.T, search_texts_across, preferred_element_type=jnp.float32)
        passage_grads = passage_grads + rounded(document_contribution)
    losses = jnp.concatenate(loss_parts, axis=1).reshape(N_BLK * N_GRP * QC)
    query_grads = jnp.concatenate(grad_parts, axis=1).reshape(N_BLK * N_GRP, QC, D)
    cotangent = query_grads[:, :SUB_DEV].reshape(S, D).astype(jnp.bfloat16)
    hidden_f = last_hidden.astype(jnp.float32)
    inv_rms = lax.rsqrt(lax.optimization_barrier(jnp.mean(hidden_f * hidden_f, axis=1, keepdims=True)) + epsilon)
    gain_row = norm_gain.astype(jnp.float32)
    normed = (hidden_f * inv_rms * gain_row).astype(jnp.bfloat16)
    gate_value = matmul(normed, gate_weight)
    up_value = matmul(normed, up_weight)
    gate_sigmoid = jax.nn.sigmoid(gate_value)
    act_grad = matmul(cotangent, down_weight.T)
    up_grad = (act_grad * gate_value * gate_sigmoid).astype(jnp.bfloat16)
    gate_grad = (act_grad * up_value * gate_sigmoid * (1.0 + gate_value * (1.0 - gate_sigmoid))).astype(jnp.bfloat16)
    normed_grad = matmul(gate_grad, gate_weight.T) + matmul(up_grad, up_weight.T)
    scaled = normed_grad * gain_row
    hidden_grads = cotangent.astype(jnp.float32) + inv_rms * scaled - hidden_f * inv_rms * inv_rms * inv_rms * lax.optimization_barrier(jnp.mean(hidden_f * scaled, axis=1, keepdims=True))
    return (losses, passage_grads, hidden_grads)
```

```python
import functools

import jax
import jax.numpy as jnp
from jax import lax
from jax.experimental import pallas as pl
from jax.experimental.pallas import tpu as pltpu
from jax.sharding import PartitionSpec as P

sharpness_scale = 20.0
epsilon = 1e-06
contract_last = (((1,), (1,)), ((), ()))
MESH = pl.DeviceIdType.MESH
VM = pl.BlockSpec(memory_space=pltpu.VMEM)
DMA = pltpu.SemaphoreType.DMA
f32, bf16 = jnp.float32, jnp.bfloat16


def remote(src, dst, ssem, rsem, dev):
    return pltpu.make_async_remote_copy(
        src_ref=src, dst_ref=dst, send_sem=ssem, recv_sem=rsem, device_id=dev, device_id_type=MESH
    )


def params(cid):
    return pltpu.CompilerParams(collective_id=cid, has_side_effects=True)


def gather_kernel(nb, ng, q_ref, pos_ref, nrm_ref, all_ref, allpos_ref, allnrm_ref,
                  loc_sem, ssem, rsem, psend, precv, nsend, nrecv):
    b, g = lax.axis_index("blk"), lax.axis_index("grp")
    n, me = nb * ng, b * ng + g
    np_, zz, core = nb // 2, b // 2, b % 2
    half = q_ref.shape[0] // 2
    barrier = pltpu.get_barrier_semaphore()

    def greet(k, c):
        p = lax.rem(me + k, n)
        pl.semaphore_signal(barrier, inc=1, device_id=(p // ng, p % ng), device_id_type=MESH)
        return c

    lax.fori_loop(1, n, greet, 0)
    pl.semaphore_wait(barrier, n - 1)

    def small(k):
        p = lax.rem(me + k, n)
        dev = (p // ng, p % ng)
        return (
            remote(nrm_ref.at[p % ng], allnrm_ref.at[me], nsend.at[k], nrecv.at[k], dev),
            remote(pos_ref, allpos_ref.at[me], psend.at[k], precv.at[k], dev),
        )

    def start_small(k, c):
        for cp in small(k):
            cp.start()
        return c

    lax.fori_loop(1, n, start_small, 0)
    own = pltpu.make_async_copy(q_ref, all_ref.at[me], loc_sem)
    own.start()

    started = []

    def slot(k, gg, cc):
        return (lax.rem(zz - k + np_, np_) * 2 + cc) * ng + gg

    def send(i, src, dst, dev):
        cp = remote(src, dst, ssem.at[i], rsem.at[i], dev)
        cp.start()
        started.append(cp)

    def await_recv(i, region):
        remote(region, region, ssem.at[i], rsem.at[i], (b, g ^ 1)).wait_recv()

    A, B = pl.ds(0, half), pl.ds(half, half)
    Z, XA, XB, YA, YB, DA, DB, P0, P1, P2, P3 = [i * np_ for i in range(11)]
    xdev, ydev, pdev = (b, g ^ 1), (b, g ^ 2), (b ^ 1, g)

    for k in range(1, np_):
        send(Z + k, q_ref, all_ref.at[me], (lax.rem(zz + k, np_) * 2 + core, g))

    def column(k):
        s = slot(k, g, core)
        if k == 0:
            src, pa, pb = q_ref, q_ref.at[A], q_ref.at[B]
        else:
            await_recv(Z + k, all_ref.at[s])
            src = all_ref.at[s]
            pa, pb = all_ref.at[s, A], all_ref.at[s, B]
        send(XA + k, pa, all_ref.at[s, A], xdev)
        send(YB + k, pb, all_ref.at[s, B], ydev)
        send(XB + k, pb, all_ref.at[s, B], xdev)
        send(YA + k, pa, all_ref.at[s, A], ydev)
        send(P0 + k, src, all_ref.at[s], pdev)

    def forward(k):
        sx, sy = slot(k, g ^ 1, core), slot(k, g ^ 2, core)
        await_recv(XA + k, all_ref.at[sx, A])
        send(DA + k, all_ref.at[sx, A], all_ref.at[sx, A], ydev)
        await_recv(YB + k, all_ref.at[sy, B])
        send(DB + k, all_ref.at[sy, B], all_ref.at[sy, B], xdev)

    def share(k):
        sx, sy = slot(k, g ^ 1, core), slot(k, g ^ 2, core)
        await_recv(XB + k, all_ref.at[sx, B])
        send(P1 + k, all_ref.at[sx], all_ref.at[sx], pdev)
        await_recv(YA + k, all_ref.at[sy, A])
        send(P2 + k, all_ref.at[sy], all_ref.at[sy], pdev)

    def share_diag(k):
        sd = slot(k, g ^ 3, core)
        await_recv(DA + k, all_ref.at[sd, A])
        await_recv(DB + k, all_ref.at[sd, B])
        send(P3 + k, all_ref.at[sd], all_ref.at[sd], pdev)

    for k in range(np_):
        column(k)
        if k >= 1:
            forward(k - 1)
            share(k - 1)
    forward(np_ - 1)
    share(np_ - 1)
    for k in range(np_):
        share_diag(k)
    oc = 1 - core
    for k in range(np_):
        for base, gg in ((P0, g), (P1, g ^ 1), (P2, g ^ 2), (P3, g ^ 3)):
            await_recv(base + k, all_ref.at[slot(k, gg, oc)])
    own.wait()
    for cp in started:
        cp.wait_send()
    allnrm_ref[me] = nrm_ref[g]
    allpos_ref[me] = pos_ref[...]

    def end_small(k, c):
        for cp in small(k):
            cp.wait()
        return c

    lax.fori_loop(1, n, end_small, 0)


def gather_all(nb, ng, queries, pos, normed):
    n, np_ = nb * ng, nb // 2
    return pl.pallas_call(
        functools.partial(gather_kernel, nb, ng),
        out_shape=(
            jax.ShapeDtypeStruct((n,) + queries.shape, queries.dtype),
            jax.ShapeDtypeStruct((n,) + pos.shape, pos.dtype),
            jax.ShapeDtypeStruct((n,) + normed.shape[1:], normed.dtype),
        ),
        in_specs=[VM] * 3,
        out_specs=(pl.BlockSpec(memory_space=pl.ANY), VM, VM),
        scratch_shapes=[DMA, DMA((11 * np_,)), DMA((11 * np_,)),
                        DMA((n,)), DMA((n,)), DMA((n,)), DMA((n,))],
        compiler_params=params(0),
    )(queries, pos, normed)


def peer(axis, b, g, p):
    return (p, g) if axis == "blk" else (b, p)


def greet_axes(nb, ng, axes):
    b, g = lax.axis_index("blk"), lax.axis_index("grp")
    barrier = pltpu.get_barrier_semaphore()
    total = 0
    for axis, n, me in (("blk", nb, b), ("grp", ng, g)):
        if axis in axes:
            for k in range(1, n):
                pl.semaphore_signal(barrier, inc=1, device_id=peer(axis, b, g, lax.rem(me + k, n)),
                                    device_id_type=MESH)
            total += n - 1
    pl.semaphore_wait(barrier, total)
    return b, g


def reduce_kernel(nb, ng, axis, x_ref, out_ref, buf, s1, r1, s2, r2):
    b, g = greet_axes(nb, ng, (axis,))
    n, me = (nb, b) if axis == "blk" else (ng, g)
    first = []
    for k in range(1, n):
        p = lax.rem(me + k, n)
        cp = remote(x_ref.at[p], buf.at[k], s1.at[k], r1.at[k], peer(axis, b, g, p))
        cp.start()
        first.append(cp)
    acc = x_ref[me].astype(f32)
    for k in range(1, n):
        first[k - 1].wait_recv()
        acc = acc + buf[k].astype(f32)
    out_ref[me] = acc.astype(out_ref.dtype)
    second = []
    for k in range(1, n):
        cp = remote(out_ref.at[me], out_ref.at[me], s2.at[k], r2.at[k],
                    peer(axis, b, g, lax.rem(me + k, n)))
        cp.start()
        second.append(cp)
    for cp in first:
        cp.wait_send()
    for k in range(1, n):
        src = lax.rem(me - k + n, n)
        remote(out_ref.at[src], out_ref.at[src], s2.at[k], r2.at[k], peer(axis, b, g, src)).wait_recv()
    for cp in second:
        cp.wait_send()


def reduce_all(nb, ng, axis, x, cid):
    n = nb if axis == "blk" else ng
    return pl.pallas_call(
        functools.partial(reduce_kernel, nb, ng, axis),
        out_shape=jax.ShapeDtypeStruct(x.shape, x.dtype),
        in_specs=[VM],
        out_specs=VM,
        scratch_shapes=[pltpu.VMEM(x.shape, x.dtype), DMA((n,)), DMA((n,)), DMA((n,)), DMA((n,))],
        compiler_params=params(cid),
    )(x)


def combine(buf, n):
    top = buf[0, 0]
    for k in range(1, n):
        top = jnp.maximum(top, buf[k, 0])
    total, hit = jnp.zeros_like(top), jnp.zeros_like(top)
    for k in range(n):
        total = total + buf[k, 1] * jnp.exp(buf[k, 0] - top)
        hit = hit + buf[k, 2]
    return top, total, hit


def stats_kernel(nb, ng, x_ref, out_ref, buf1, buf2, s1, r1, s2, r2):
    b, g = greet_axes(nb, ng, ("blk", "grp"))
    copies = []
    for k in range(1, ng):
        cp = remote(x_ref, buf1.at[g], s1.at[k], r1.at[k], (b, lax.rem(g + k, ng)))
        cp.start()
        copies.append(cp)
    buf1[g] = x_ref[...]
    for cp in copies:
        cp.wait()
    for i, v in enumerate(combine(buf1, ng)):
        buf2[b, i] = v
    copies = []
    for k in range(1, nb):
        cp = remote(buf2.at[b], buf2.at[b], s2.at[k], r2.at[k], (lax.rem(b + k, nb), g))
        cp.start()
        copies.append(cp)
    for cp in copies:
        cp.wait()
    top, total, hit = combine(buf2, nb)
    out_ref[0] = top + jnp.log(total)
    out_ref[1] = hit


def share_stats(nb, ng, x):
    return pl.pallas_call(
        functools.partial(stats_kernel, nb, ng),
        out_shape=jax.ShapeDtypeStruct((2,) + x.shape[1:], f32),
        in_specs=[VM],
        out_specs=VM,
        scratch_shapes=[pltpu.VMEM((ng,) + x.shape, f32), pltpu.VMEM((nb,) + x.shape, f32),
                        DMA((ng,)), DMA((ng,)), DMA((nb,)), DMA((nb,))],
        compiler_params=params(2),
    )(x)


def finish_kernel(nb, ng, x_ref, cot_ref, out_ref, cots_ref, buf, acc, s1, r1, s2, r2, s3, r3):
    b, g = greet_axes(nb, ng, ("blk", "grp"))
    rest = []
    for k in range(1, ng):
        p = lax.rem(g + k, ng)
        cp = remote(cot_ref.at[p], cots_ref.at[g], s3.at[k], r3.at[k], (b, p))
        cp.start()
        rest.append(cp)
    first = []
    for k in range(1, nb):
        p = lax.rem(b + k, nb)
        cp = remote(x_ref.at[p], buf.at[k], s1.at[k], r1.at[k], (p, g))
        cp.start()
        first.append(cp)
    total = x_ref[b].astype(f32)
    for k in range(1, nb):
        first[k - 1].wait_recv()
        total = total + buf[k].astype(f32)
    acc[...] = total
    for k in range(1, ng):
        p = lax.rem(g + k, ng)
        cp = remote(acc.at[p], out_ref.at[g], s2.at[k], r2.at[k], (b, p))
        cp.start()
        rest.append(cp)
    out_ref[g] = acc[g]
    cots_ref[g] = cot_ref[g]
    for cp in first:
        cp.wait_send()
    for cp in rest:
        cp.wait()


def finish(nb, ng, x, cot):
    return pl.pallas_call(
        functools.partial(finish_kernel, nb, ng),
        out_shape=(jax.ShapeDtypeStruct(cot.shape, f32),) * 2,
        in_specs=[VM] * 2,
        out_specs=(VM, VM),
        scratch_shapes=[pltpu.VMEM(x.shape, x.dtype), pltpu.VMEM(cot.shape, f32),
                        DMA((nb,)), DMA((nb,)), DMA((ng,)), DMA((ng,)), DMA((ng,)), DMA((ng,))],
        compiler_params=params(5),
    )(x, cot)


def row_norm(hidden):
    hidden_f = hidden.astype(f32)
    inv_rms = lax.rsqrt(jnp.mean(hidden_f * hidden_f, axis=1, keepdims=True) + epsilon)
    return (hidden_f, inv_rms)


def swiglu_grads(act_grad, gate_value, up_value):
    gate_sigmoid = jax.nn.sigmoid(gate_value)
    up_grad = (act_grad * gate_value * gate_sigmoid).astype(bf16)
    gate_grad = (
        act_grad * up_value * gate_sigmoid * (1.0 + gate_value * (1.0 - gate_sigmoid))
    ).astype(bf16)
    return (up_grad, gate_grad)


def shards(nb, ng, queries, docs, positive, last_hidden, norm_gain, gate_weight, up_weight, down_weight):
    b, g = lax.axis_index("blk"), lax.axis_index("grp")
    n, (rows, width) = nb * ng, queries.shape
    total_rows = n * rows
    sub = last_hidden.shape[0]
    sub_all = sub * n
    feat, hidden_units = gate_weight.shape
    shard_rows = docs.shape[0]
    own_docs = shard_rows // ng

    hidden_f, inv_rms = row_norm(last_hidden)
    normed = (hidden_f * inv_rms * norm_gain).astype(bf16)
    normed = normed.reshape(sub, ng, feat).transpose(1, 0, 2)
    pos = jnp.pad(positive.reshape(1, rows), ((0, 0), (0, 128 - rows)))
    all_q, all_pos, all_normed = gather_all(nb, ng, queries, pos, normed)
    q = all_q.reshape(total_rows, width)
    pos = all_pos[:, 0, :rows].reshape(total_rows)
    normed_part = all_normed.reshape(sub_all, feat)

    per = sub_all // ng
    gate_part = jnp.dot(normed_part, gate_weight, preferred_element_type=f32).astype(bf16)
    up_part = jnp.dot(normed_part, up_weight, preferred_element_type=f32).astype(bf16)
    both = jnp.concatenate(
        [gate_part.reshape(ng, per, hidden_units), up_part.reshape(ng, per, hidden_units)], axis=1
    )
    both = reduce_all(nb, ng, "grp", both, 1)
    gate_value = both[:, :per].reshape(sub_all, hidden_units).astype(f32)
    up_value = both[:, per:].reshape(sub_all, hidden_units).astype(f32)

    mine = lax.dynamic_slice_in_dim(docs, g * own_docs, own_docs)
    scores = sharpness_scale * lax.dot_general(mine, q, contract_last, preferred_element_type=f32)
    ids = lax.broadcasted_iota(jnp.int32, (own_docs, 1), 0) + (b * shard_rows + g * own_docs)
    hits = ids == pos[None, :]
    top = jnp.max(scores, axis=0)
    summed = jnp.sum(jnp.exp(scores - top[None, :]), axis=0)
    hit = jnp.sum(jnp.where(hits, scores, 0.0), axis=0)
    stats = jnp.stack([top, summed, hit]).reshape(3, total_rows // 128, 128)
    done = share_stats(nb, ng, stats).reshape(2, total_rows)
    log_total, pos_logit = done[0], done[1]
    losses = lax.dynamic_slice_in_dim(log_total - pos_logit, (b * ng + g) * rows, rows)
    weights = (jnp.exp(scores - log_total[None, :]) - hits.astype(f32)).astype(bf16)
    passage_grads = sharpness_scale * jnp.dot(weights, q, preferred_element_type=f32)

    sub_q = all_q[:, :sub].reshape(sub_all, width)
    sub_scores = sharpness_scale * lax.dot_general(sub_q, docs, contract_last, preferred_element_type=f32)
    sub_total = log_total.reshape(n, rows)[:, :sub].reshape(sub_all)
    sub_pos = pos.reshape(n, rows)[:, :sub].reshape(sub_all)
    sub_ids = lax.broadcasted_iota(jnp.int32, (1, shard_rows), 1) + b * shard_rows
    sub_hits = sub_ids == sub_pos[:, None]
    sub_weights = (jnp.exp(sub_scores - sub_total[:, None]) - sub_hits.astype(f32)).astype(bf16)
    doc_part = lax.dynamic_slice_in_dim(docs, g * feat, feat, 1)
    cot_part = (sharpness_scale * jnp.dot(sub_weights, doc_part, preferred_element_type=f32)).astype(bf16)
    cot = reduce_all(nb, ng, "blk", cot_part.reshape(nb, sub * ng, feat), 3)
    cot_own = lax.dynamic_index_in_dim(cot, b, 0, keepdims=False).reshape(ng, sub, feat).astype(f32)
    cot = cot.reshape(sub_all, feat)

    act_part = lax.dot_general(cot, down_weight, contract_last, preferred_element_type=f32).astype(bf16)
    act_grad = reduce_all(nb, ng, "grp", act_part.reshape(ng, per, hidden_units), 4)
    act_grad = act_grad.reshape(sub_all, hidden_units).astype(f32)
    up_grad, gate_grad = swiglu_grads(act_grad, gate_value, up_value)
    from_gate = lax.dot_general(gate_grad, gate_weight, contract_last, preferred_element_type=f32)
    from_up = lax.dot_general(up_grad, up_weight, contract_last, preferred_element_type=f32)
    share = (from_gate + from_up).astype(bf16).reshape(nb, ng, sub, feat)
    normed_grad, cots = finish(nb, ng, share, cot_own)
    normed_grad = normed_grad.transpose(1, 0, 2).reshape(sub, width)
    cots = cots.transpose(1, 0, 2).reshape(sub, width)
    scaled = normed_grad * norm_gain
    hidden_grads = (
        cots
        + inv_rms * scaled
        - hidden_f
        * inv_rms
        * inv_rms
        * inv_rms
        * jnp.mean(hidden_f * scaled, axis=1, keepdims=True)
    )
    return (losses, passage_grads, hidden_grads)


def solution(mesh):
    return jax.shard_map(
        functools.partial(shards, mesh.shape["blk"], mesh.shape["grp"]),
        mesh=mesh,
        in_specs=(
            P(("blk", "grp"), None),
            P("blk", None),
            P(("blk", "grp")),
            P(("blk", "grp"), None),
            P(),
            P("grp", "blk"),
            P("grp", "blk"),
            P("blk", "grp"),
        ),
        out_specs=(P(("blk", "grp")), P(("blk", "grp"), None), P(("blk", "grp"), None)),
        check_vma=False,
    )
```

```python
import functools

import jax
import jax.numpy as jnp
from jax import lax
from jax.experimental import pallas as pl
from jax.experimental.pallas import tpu as pltpu
from jax.sharding import PartitionSpec as P

sharpness_scale = 20.0
epsilon = 1e-06
contract_last = (((1,), (1,)), ((), ()))
MESH = pl.DeviceIdType.MESH
VM = pl.BlockSpec(memory_space=pltpu.VMEM)
DMA = pltpu.SemaphoreType.DMA
f32, bf16 = jnp.float32, jnp.bfloat16


def remote(src, dst, ssem, rsem, dev):
    return pltpu.make_async_remote_copy(
        src_ref=src, dst_ref=dst, send_sem=ssem, recv_sem=rsem, device_id=dev, device_id_type=MESH
    )


def params(cid):
    return pltpu.CompilerParams(collective_id=cid, has_side_effects=True)


def main_kernel(nb, ng, q_ref, pos_ref, nrm_ref, subq_ref, spos_ref, docs_hbm, gate_hbm, up_hbm, down_hbm,
                all_ref, allpos_ref, grad_ref, cots_ref,
                allnrm, allsub, allspos, docs, gate, up, down, rows_f, nrm_f,
                gu_x, gu_buf, gu_out, st_buf, cot_x, cot_buf, cot_out, cot_f, act_x, act_buf, act_out,
                gg, ug, fin_x, fin_buf, piece, cpiece, scores,
                loc_sem, ssem, rsem, small_s, small_r):
    b, g = lax.axis_index("blk"), lax.axis_index("grp")
    n, me = nb * ng, b * ng + g
    np_, zz, core = nb // 2, b // 2, b % 2
    half = q_ref.shape[0] // 2
    sub = subq_ref.shape[0]
    sub_all, feat, block = sub * n, gate.shape[0], sub * ng
    per = sub_all // ng
    barrier = pltpu.get_barrier_semaphore()

    def greet(k, c):
        p = lax.rem(me + k, n)
        pl.semaphore_signal(barrier, inc=1, device_id=(p // ng, p % ng), device_id_type=MESH)
        return c

    local = []
    for i, (src, dst) in enumerate(((gate_hbm, gate), (up_hbm, up), (docs_hbm, docs), (down_hbm, down))):
        cp = pltpu.make_async_copy(src, dst, loc_sem.at[i + 1])
        cp.start()
        local.append(cp)
    lax.fori_loop(1, n, greet, 0)
    pl.semaphore_wait(barrier, n - 1)

    def small(i, k):
        p = lax.rem(me + k, n)
        src, dst = ((nrm_ref.at[p % ng], allnrm), (subq_ref, allsub),
                    (spos_ref, allspos), (pos_ref, allpos_ref))[i]
        return remote(src, dst.at[me], small_s.at[i, k], small_r.at[i, k], (p // ng, p % ng))

    def over_small(which, act):
        def go(k, c):
            act(small(which, k))
            return c
        lax.fori_loop(1, n, go, 0)

    for i in range(4):
        over_small(i, lambda cp: cp.start())
    own = pltpu.make_async_copy(q_ref, all_ref.at[me], loc_sem.at[0])
    own.start()
    allnrm[me] = nrm_ref[g]
    allsub[me] = subq_ref[...]
    allspos[me] = spos_ref[...]
    allpos_ref[me] = pos_ref[...]

    started = []

    def slot(k, gg_, cc):
        return (lax.rem(zz - k + np_, np_) * 2 + cc) * ng + gg_

    def send(i, src, dst, dev):
        cp = remote(src, dst, ssem.at[i], rsem.at[i], dev)
        cp.start()
        started.append(cp)

    def await_recv(i, region):
        remote(region, region, ssem.at[i], rsem.at[i], (b, g ^ 1)).wait_recv()

    A, B = pl.ds(0, half), pl.ds(half, half)
    Z, XA, XB, YA, YB, DA, DB, P0, P1, P2, P3, base = [i * np_ for i in range(12)]
    xdev, ydev, pdev = (b, g ^ 1), (b, g ^ 2), (b ^ 1, g)

    def column(k):
        s = slot(k, g, core)
        if k == 0:
            src, pa, pb = q_ref, q_ref.at[A], q_ref.at[B]
        else:
            await_recv(Z + k, all_ref.at[s])
            src = all_ref.at[s]
            pa, pb = all_ref.at[s, A], all_ref.at[s, B]
        send(XA + k, pa, all_ref.at[s, A], xdev)
        send(YB + k, pb, all_ref.at[s, B], ydev)
        send(XB + k, pb, all_ref.at[s, B], xdev)
        send(YA + k, pa, all_ref.at[s, A], ydev)
        send(P0 + k, src, all_ref.at[s], pdev)

    def forward(k):
        sx, sy = slot(k, g ^ 1, core), slot(k, g ^ 2, core)
        await_recv(XA + k, all_ref.at[sx, A])
        send(DA + k, all_ref.at[sx, A], all_ref.at[sx, A], ydev)
        await_recv(YB + k, all_ref.at[sy, B])
        send(DB + k, all_ref.at[sy, B], all_ref.at[sy, B], xdev)

    def share(k):
        sx, sy = slot(k, g ^ 1, core), slot(k, g ^ 2, core)
        await_recv(XB + k, all_ref.at[sx, B])
        send(P1 + k, all_ref.at[sx], all_ref.at[sx], pdev)
        await_recv(YA + k, all_ref.at[sy, A])
        send(P2 + k, all_ref.at[sy], all_ref.at[sy], pdev)

    def share_diag(k):
        sd = slot(k, g ^ 3, core)
        await_recv(DA + k, all_ref.at[sd, A])
        await_recv(DB + k, all_ref.at[sd, B])
        send(P3 + k, all_ref.at[sd], all_ref.at[sd], pdev)

    bulk = [functools.partial(column, k) for k in range(1, 2)]
    for k in range(2, np_):
        bulk += [functools.partial(column, k), functools.partial(forward, k - 2)]
    for k in range(max(np_ - 2, 0), np_):
        bulk += [functools.partial(forward, k)]
    bulk += [functools.partial(share, k) for k in range(np_)]
    bulk += [functools.partial(share_diag, k) for k in range(np_)]

    def advance(count):
        for _ in range(min(count, len(bulk))):
            bulk.pop(0)()

    G1, G2 = base, base + ng
    A1, A2 = G2 + ng, G2 + 2 * ng
    F2, F3 = A2 + ng, A2 + 2 * ng
    S1 = F3 + ng
    C1, C2, F1 = S1 + nb, S1 + 2 * nb, S1 + 3 * nb
    lines = {"grp": (ng, g), "blk": (nb, b)}

    def at(axis, p):
        return (p, g) if axis == "blk" else (b, p)

    def scatter(axis, i, x, buf):
        count, mine = lines[axis]
        for k in range(1, count):
            p = lax.rem(mine + k, count)
            send(i + k, x.at[p], buf.at[k], at(axis, p))

    def collect(axis, i, x, buf):
        count, mine = lines[axis]
        acc = x[mine].astype(f32)
        for k in range(1, count):
            await_recv(i + k, buf.at[k])
            acc = acc + buf[k].astype(f32)
        return acc

    def spread(axis, i, out):
        count, mine = lines[axis]
        for k in range(1, count):
            send(i + k, out.at[mine], out.at[mine], at(axis, lax.rem(mine + k, count)))

    def await_spread(axis, i, out):
        count, mine = lines[axis]
        for k in range(1, count):
            await_recv(i + k, out.at[lax.rem(mine - k + count, count)])

    for k in range(1, np_):
        send(Z + k, q_ref, all_ref.at[me], (lax.rem(zz + k, np_) * 2 + core, g))
    column(0)

    over_small(0, lambda cp: cp.wait())
    for i in range(n):
        nrm_f[i * sub:(i + 1) * sub] = allnrm[i].astype(f32)
    normed = nrm_f[...].astype(bf16)
    for i, (w, cp) in enumerate(((gate, local[0]), (up, local[1]))):
        cp.wait()
        part = jnp.dot(normed, w[...], preferred_element_type=f32).astype(bf16)
        for j in range(ng):
            gu_x[j, i * per:(i + 1) * per] = part[j * per:(j + 1) * per]
    scatter("grp", G1, gu_x, gu_buf)
    advance(1)

    over_small(1, lambda cp: cp.wait())
    over_small(2, lambda cp: cp.wait())
    for i in range(n):
        rows_f[i * sub:(i + 1) * sub] = allsub[i].astype(f32)
    sub_q = rows_f[...].astype(bf16)
    local[2].wait()
    count = docs.shape[0]
    tile = 256 if count % 256 == 0 else count

    def score(i, c):
        at_rows = pl.ds(pl.multiple_of(i * tile, tile), tile)
        scores[at_rows] = sharpness_scale * lax.dot_general(
            docs[at_rows], sub_q, contract_last, preferred_element_type=f32)
        return c

    lax.fori_loop(0, count // tile, score, 0)
    sc = scores[...]
    top = jnp.max(sc, axis=0, keepdims=True)
    st_buf[b] = jnp.zeros(st_buf.shape[1:], f32)
    st_buf[b, 0:1] = top
    st_buf[b, 1:2] = jnp.sum(jnp.exp(sc - top), axis=0, keepdims=True)
    spread("blk", S1, st_buf)
    gu_out[g] = collect("grp", G1, gu_x, gu_buf).astype(bf16)
    spread("grp", G2, gu_out)
    await_spread("blk", S1, st_buf)
    high = st_buf[0, 0:1]
    for k in range(1, nb):
        high = jnp.maximum(high, st_buf[k, 0:1])
    total = jnp.zeros_like(high)
    for k in range(nb):
        total = total + st_buf[k, 1:2] * jnp.exp(st_buf[k, 0:1] - high)
    log_total = high + jnp.log(total)
    where = allspos[0]
    for k in range(1, n):
        where = where + allspos[k]
    ids = lax.broadcasted_iota(jnp.int32, sc.shape, 0) + b * count
    weights = (jnp.exp(sc - log_total) - (ids == where[:, :sub_all]).astype(f32)).astype(bf16)
    doc_part = docs[:, pl.ds(pl.multiple_of(g * feat, 128), feat)]
    part = sharpness_scale * lax.dot_general(
        weights, doc_part, (((0,), (0,)), ((), ())), preferred_element_type=f32)
    for p in range(nb):
        cot_x[p] = part[p * block:(p + 1) * block].astype(bf16)
    scatter("blk", C1, cot_x, cot_buf)
    advance(2)
    mine = collect("blk", C1, cot_x, cot_buf).astype(bf16)
    cot_out[b] = mine
    spread("blk", C2, cot_out)
    mine_f = mine.astype(f32)
    for j in range(ng):
        cpiece[j] = mine_f[j * sub:(j + 1) * sub]
    for k in range(1, ng):
        p = lax.rem(g + k, ng)
        send(F3 + k, cpiece.at[p], cots_ref.at[g], (b, p))
    await_spread("blk", C2, cot_out)
    for p in range(nb):
        cot_f[p * block:(p + 1) * block] = cot_out[p].astype(f32)
    local[3].wait()
    part = lax.dot_general(cot_f[...].astype(bf16), down[...], contract_last, preferred_element_type=f32)
    for j in range(ng):
        act_x[j] = part[j * per:(j + 1) * per].astype(bf16)
    scatter("grp", A1, act_x, act_buf)
    act_out[g] = collect("grp", A1, act_x, act_buf).astype(bf16)
    spread("grp", A2, act_out)
    advance(2)
    await_spread("grp", G2, gu_out)
    await_spread("grp", A2, act_out)
    for j in range(ng):
        u_grad, g_grad = swiglu_grads(
            act_out[j].astype(f32), gu_out[j, 0:per].astype(f32), gu_out[j, per:2 * per].astype(f32))
        gg[j * per:(j + 1) * per] = g_grad
        ug[j * per:(j + 1) * per] = u_grad
    part = lax.dot_general(gg[...], gate[...], contract_last, preferred_element_type=f32)
    part = part + lax.dot_general(ug[...], up[...], contract_last, preferred_element_type=f32)
    for p in range(nb):
        fin_x[p] = part[p * block:(p + 1) * block].astype(bf16)
    scatter("blk", F1, fin_x, fin_buf)
    advance(2)
    done = collect("blk", F1, fin_x, fin_buf)
    for j in range(ng):
        piece[j] = done[j * sub:(j + 1) * sub]
    for k in range(1, ng):
        p = lax.rem(g + k, ng)
        send(F2 + k, piece.at[p], grad_ref.at[g], (b, p))
    grad_ref[g] = piece[g]
    cots_ref[g] = cpiece[g]
    advance(len(bulk))
    oc = 1 - core
    for k in range(np_):
        for start, gx in ((P0, g), (P1, g ^ 1), (P2, g ^ 2), (P3, g ^ 3)):
            await_recv(start + k, all_ref.at[slot(k, gx, oc)])
    await_spread("grp", F2, grad_ref)
    await_spread("grp", F3, cots_ref)
    own.wait()
    over_small(3, lambda cp: cp.wait())
    for cp in started:
        cp.wait_send()


def run_main(nb, ng, queries, pos, normed, subq, spos, docs, gate, up, down):
    n, np_ = nb * ng, nb // 2
    sub = subq.shape[0]
    feat, hidden = gate.shape
    sub_all, block = sub * n, sub * ng
    per = sub_all // ng
    sems = 12 * np_ + 6 * ng + 4 * nb
    V = pltpu.VMEM
    any_ = pl.BlockSpec(memory_space=pl.ANY)
    return pl.pallas_call(
        functools.partial(main_kernel, nb, ng),
        out_shape=(
            jax.ShapeDtypeStruct((n,) + queries.shape, queries.dtype),
            jax.ShapeDtypeStruct((n,) + pos.shape, pos.dtype),
            jax.ShapeDtypeStruct((ng, sub, feat), f32),
            jax.ShapeDtypeStruct((ng, sub, feat), f32),
        ),
        in_specs=[VM] * 5 + [any_] * 4,
        out_specs=(any_, VM, VM, VM),
        scratch_shapes=[
            V((n, sub, feat), bf16), V((n,) + subq.shape, bf16), V((n,) + spos.shape, jnp.int32),
            V(docs.shape, bf16), V(gate.shape, bf16), V(up.shape, bf16), V(down.shape, bf16),
            V((sub_all, queries.shape[1]), f32), V((sub_all, feat), f32),
            V((ng, 2 * per, hidden), bf16), V((ng, 2 * per, hidden), bf16), V((ng, 2 * per, hidden), bf16),
            V((nb, 8, sub_all), f32),
            V((nb, block, feat), bf16), V((nb, block, feat), bf16), V((nb, block, feat), bf16),
            V((sub_all, feat), f32),
            V((ng, per, hidden), bf16), V((ng, per, hidden), bf16), V((ng, per, hidden), bf16),
            V((sub_all, hidden), bf16), V((sub_all, hidden), bf16),
            V((nb, block, feat), bf16), V((nb, block, feat), bf16),
            V((ng, sub, feat), f32), V((ng, sub, feat), f32),
            V((docs.shape[0], sub_all), f32),
            DMA((5,)), DMA((sems,)), DMA((sems,)), DMA((4, n)), DMA((4, n)),
        ],
        compiler_params=params(0),
    )(queries, pos, normed, subq, spos, docs, gate, up, down)


def peer(axis, b, g, p):
    return (p, g) if axis == "blk" else (b, p)


def greet_axes(nb, ng, axes):
    b, g = lax.axis_index("blk"), lax.axis_index("grp")
    barrier = pltpu.get_barrier_semaphore()
    total = 0
    for axis, n, me in (("blk", nb, b), ("grp", ng, g)):
        if axis in axes:
            for k in range(1, n):
                pl.semaphore_signal(barrier, inc=1, device_id=peer(axis, b, g, lax.rem(me + k, n)),
                                    device_id_type=MESH)
            total += n - 1
    pl.semaphore_wait(barrier, total)
    return b, g


def combine(buf, n):
    top = buf[0, 0]
    for k in range(1, n):
        top = jnp.maximum(top, buf[k, 0])
    total, hit = jnp.zeros_like(top), jnp.zeros_like(top)
    for k in range(n):
        total = total + buf[k, 1] * jnp.exp(buf[k, 0] - top)
        hit = hit + buf[k, 2]
    return top, total, hit


def stats_kernel(nb, ng, x_ref, out_ref, buf1, buf2, s1, r1, s2, r2):
    b, g = greet_axes(nb, ng, ("blk", "grp"))
    copies = []
    for k in range(1, ng):
        cp = remote(x_ref, buf1.at[g], s1.at[k], r1.at[k], (b, lax.rem(g + k, ng)))
        cp.start()
        copies.append(cp)
    buf1[g] = x_ref[...]
    for cp in copies:
        cp.wait()
    for i, v in enumerate(combine(buf1, ng)):
        buf2[b, i] = v
    copies = []
    for k in range(1, nb):
        cp = remote(buf2.at[b], buf2.at[b], s2.at[k], r2.at[k], (lax.rem(b + k, nb), g))
        cp.start()
        copies.append(cp)
    for cp in copies:
        cp.wait()
    top, total, hit = combine(buf2, nb)
    out_ref[0] = top + jnp.log(total)
    out_ref[1] = hit


def share_stats(nb, ng, x):
    return pl.pallas_call(
        functools.partial(stats_kernel, nb, ng),
        out_shape=jax.ShapeDtypeStruct((2,) + x.shape[1:], f32),
        in_specs=[VM],
        out_specs=VM,
        scratch_shapes=[pltpu.VMEM((ng,) + x.shape, f32), pltpu.VMEM((nb,) + x.shape, f32),
                        DMA((ng,)), DMA((ng,)), DMA((nb,)), DMA((nb,))],
        compiler_params=params(2),
    )(x)


def row_norm(hidden):
    hidden_f = hidden.astype(f32)
    inv_rms = lax.rsqrt(jnp.mean(hidden_f * hidden_f, axis=1, keepdims=True) + epsilon)
    return (hidden_f, inv_rms)


def swiglu_grads(act_grad, gate_value, up_value):
    gate_sigmoid = jax.nn.sigmoid(gate_value)
    up_grad = (act_grad * gate_value * gate_sigmoid).astype(bf16)
    gate_grad = (
        act_grad * up_value * gate_sigmoid * (1.0 + gate_value * (1.0 - gate_sigmoid))
    ).astype(bf16)
    return (up_grad, gate_grad)


def shards(nb, ng, queries, docs, positive, last_hidden, norm_gain, gate_weight, up_weight, down_weight):
    b, g = lax.axis_index("blk"), lax.axis_index("grp")
    n, (rows, width) = nb * ng, queries.shape
    total_rows = n * rows
    sub = last_hidden.shape[0]
    sub_all = sub * n
    feat = gate_weight.shape[0]
    shard_rows = docs.shape[0]
    own_docs = shard_rows // ng

    hidden_f, inv_rms = row_norm(last_hidden)
    normed = (hidden_f * inv_rms * norm_gain).astype(bf16)
    normed = normed.reshape(sub, ng, feat).transpose(1, 0, 2)
    pos = jnp.pad(positive.reshape(1, rows), ((0, 0), (0, 128 - rows)))
    lanes = -(-sub_all // 128) * 128
    spos = lax.dynamic_update_slice(
        jnp.zeros((1, lanes), jnp.int32), positive[:sub].reshape(1, sub), (0, (b * ng + g) * sub))
    all_q, all_pos, normed_grad, cots = run_main(
        nb, ng, queries, pos, normed, queries[:sub], spos, docs, gate_weight, up_weight, down_weight)
    q = all_q.reshape(total_rows, width)
    pos = all_pos[:, 0, :rows].reshape(total_rows)

    mine = lax.dynamic_slice_in_dim(docs, g * own_docs, own_docs)
    scores = sharpness_scale * lax.dot_general(mine, q, contract_last, preferred_element_type=f32)
    ids = lax.broadcasted_iota(jnp.int32, (own_docs, 1), 0) + (b * shard_rows + g * own_docs)
    hits = ids == pos[None, :]
    top = jnp.max(scores, axis=0)
    summed = jnp.sum(jnp.exp(scores - top[None, :]), axis=0)
    hit = jnp.sum(jnp.where(hits, scores, 0.0), axis=0)
    stats = jnp.stack([top, summed, hit]).reshape(3, total_rows // 128, 128)
    done = share_stats(nb, ng, stats).reshape(2, total_rows)
    log_total, pos_logit = done[0], done[1]
    losses = lax.dynamic_slice_in_dim(log_total - pos_logit, (b * ng + g) * rows, rows)
    weights = (jnp.exp(scores - log_total[None, :]) - hits.astype(f32)).astype(bf16)
    passage_grads = sharpness_scale * jnp.dot(weights, q, preferred_element_type=f32)

    normed_grad = normed_grad.transpose(1, 0, 2).reshape(sub, width)
    cots = cots.transpose(1, 0, 2).reshape(sub, width)
    scaled = normed_grad * norm_gain
    hidden_grads = (
        cots
        + inv_rms * scaled
        - hidden_f
        * inv_rms
        * inv_rms
        * inv_rms
        * jnp.mean(hidden_f * scaled, axis=1, keepdims=True)
    )
    return (losses, passage_grads, hidden_grads)


def solution(mesh):
    return jax.shard_map(
        functools.partial(shards, mesh.shape["blk"], mesh.shape["grp"]),
        mesh=mesh,
        in_specs=(
            P(("blk", "grp"), None),
            P("blk", None),
            P(("blk", "grp")),
            P(("blk", "grp"), None),
            P(),
            P("grp", "blk"),
            P("grp", "blk"),
            P("blk", "grp"),
        ),
        out_specs=(P(("blk", "grp")), P(("blk", "grp"), None), P(("blk", "grp"), None)),
        check_vma=False,
    )
```

```python
import functools

import jax
import jax.numpy as jnp
from jax import lax
from jax.experimental import pallas as pl
from jax.experimental.pallas import tpu as pltpu
from jax.sharding import PartitionSpec as P

sharpness_scale = 20.0
epsilon = 1e-06
contract_last = (((1,), (1,)), ((), ()))
MESH = pl.DeviceIdType.MESH
VM = pl.BlockSpec(memory_space=pltpu.VMEM)
DMA = pltpu.SemaphoreType.DMA
f32, bf16 = jnp.float32, jnp.bfloat16


def remote(src, dst, ssem, rsem, dev):
    return pltpu.make_async_remote_copy(
        src_ref=src, dst_ref=dst, send_sem=ssem, recv_sem=rsem, device_id=dev, device_id_type=MESH
    )


def params(cid):
    return pltpu.CompilerParams(collective_id=cid, has_side_effects=True)


def main_kernel(nb, ng, q_ref, pos_ref, nrm_ref, spos_ref, docs_hbm, gate_hbm, up_hbm, down_hbm,
                all_ref, allpos_ref, grad_ref, cots_ref,
                allnrm, allsub, allspos, docs, gate, up, down, rows_f, nrm_f,
                gu_x, gu_buf, gu_out, st_buf, cot_x, cot_buf, cot_out, cot_f, act_x, act_buf, act_out,
                gg, ug, fin_x, fin_buf, piece, cpiece, scores,
                subq_ref, loc_sem, ssem, rsem, small_s, small_r):
    b, g = lax.axis_index("blk"), lax.axis_index("grp")
    n, me = nb * ng, b * ng + g
    np_, zz, core = nb // 2, b // 2, b % 2
    half = q_ref.shape[0] // 2
    sub = subq_ref.shape[0]
    sub_all, feat, block = sub * n, gate.shape[1], sub * ng
    per = sub_all // ng
    barrier = pltpu.get_barrier_semaphore()
    subq_ref[...] = q_ref[0:sub]

    def greet(k, c):
        p = lax.rem(me + k, n)
        pl.semaphore_signal(barrier, inc=1, device_id=(p // ng, p % ng), device_id_type=MESH)
        return c

    local = []
    for i, (src, dst) in enumerate(((gate_hbm, gate), (up_hbm, up), (docs_hbm, docs), (down_hbm, down))):
        cp = pltpu.make_async_copy(src, dst, loc_sem.at[i + 1])
        cp.start()
        local.append(cp)
    lax.fori_loop(1, n, greet, 0)
    pl.semaphore_wait(barrier, n - 1)

    def small(i, k):
        p = lax.rem(me + k, n)
        src, dst = ((nrm_ref.at[p % ng], allnrm), (subq_ref, allsub),
                    (spos_ref, allspos), (pos_ref, allpos_ref))[i]
        return remote(src, dst.at[me], small_s.at[i, k], small_r.at[i, k], (p // ng, p % ng))

    def over_small(which, act):
        def go(k, c):
            act(small(which, k))
            return c
        lax.fori_loop(1, n, go, 0)

    for i in range(4):
        over_small(i, lambda cp: cp.start())
    own = pltpu.make_async_copy(q_ref, all_ref.at[me], loc_sem.at[0])
    own.start()
    allnrm[me] = nrm_ref[g]
    allsub[me] = subq_ref[...]
    allspos[me] = spos_ref[...]
    allpos_ref[me] = pos_ref[...]

    started = []

    def slot(k, gg_, cc):
        return (lax.rem(zz - k + np_, np_) * 2 + cc) * ng + gg_

    def send(i, src, dst, dev):
        cp = remote(src, dst, ssem.at[i], rsem.at[i], dev)
        cp.start()
        started.append(cp)

    def await_recv(i, region):
        remote(region, region, ssem.at[i], rsem.at[i], (b, g ^ 1)).wait_recv()

    A, B = pl.ds(0, half), pl.ds(half, half)
    Z, XA, XB, YA, YB, DA, DB, P0, P1, P2, P3, base = [i * np_ for i in range(12)]
    xdev, ydev, pdev = (b, g ^ 1), (b, g ^ 2), (b ^ 1, g)

    def column(k):
        s = slot(k, g, core)
        if k == 0:
            src, pa, pb = q_ref, q_ref.at[A], q_ref.at[B]
        else:
            await_recv(Z + k, all_ref.at[s])
            src = all_ref.at[s]
            pa, pb = all_ref.at[s, A], all_ref.at[s, B]
        send(XA + k, pa, all_ref.at[s, A], xdev)
        send(YB + k, pb, all_ref.at[s, B], ydev)
        send(XB + k, pb, all_ref.at[s, B], xdev)
        send(YA + k, pa, all_ref.at[s, A], ydev)
        send(P0 + k, src, all_ref.at[s], pdev)

    def forward(k):
        sx, sy = slot(k, g ^ 1, core), slot(k, g ^ 2, core)
        await_recv(XA + k, all_ref.at[sx, A])
        send(DA + k, all_ref.at[sx, A], all_ref.at[sx, A], ydev)
        await_recv(YB + k, all_ref.at[sy, B])
        send(DB + k, all_ref.at[sy, B], all_ref.at[sy, B], xdev)

    def share(k):
        sx, sy = slot(k, g ^ 1, core), slot(k, g ^ 2, core)
        await_recv(XB + k, all_ref.at[sx, B])
        send(P1 + k, all_ref.at[sx], all_ref.at[sx], pdev)
        await_recv(YA + k, all_ref.at[sy, A])
        send(P2 + k, all_ref.at[sy], all_ref.at[sy], pdev)

    def share_diag(k):
        sd = slot(k, g ^ 3, core)
        await_recv(DA + k, all_ref.at[sd, A])
        await_recv(DB + k, all_ref.at[sd, B])
        send(P3 + k, all_ref.at[sd], all_ref.at[sd], pdev)

    bulk = [functools.partial(column, k) for k in range(1, 2)]
    for k in range(2, np_):
        bulk += [functools.partial(column, k), functools.partial(forward, k - 2)]
    for k in range(max(np_ - 2, 0), np_):
        bulk += [functools.partial(forward, k)]
    bulk += [functools.partial(share, k) for k in range(np_)]
    bulk += [functools.partial(share_diag, k) for k in range(np_)]

    def advance(count):
        for _ in range(min(count, len(bulk))):
            bulk.pop(0)()

    G1, G2 = base, base + ng
    A1, A2 = G2 + ng, G2 + 2 * ng
    F2, F3 = A2 + ng, A2 + 2 * ng
    S1 = F3 + ng
    C1, C2, F1 = S1 + nb, S1 + 2 * nb, S1 + 3 * nb
    lines = {"grp": (ng, g), "blk": (nb, b)}

    def at(axis, p):
        return (p, g) if axis == "blk" else (b, p)

    def scatter(axis, i, x, buf):
        count, mine = lines[axis]
        for k in range(1, count):
            p = lax.rem(mine + k, count)
            send(i + k, x.at[p], buf.at[k], at(axis, p))

    def collect(axis, i, x, buf):
        count, mine = lines[axis]
        acc = x[mine].astype(f32)
        for k in range(1, count):
            await_recv(i + k, buf.at[k])
            acc = acc + buf[k].astype(f32)
        return acc

    def spread(axis, i, out):
        count, mine = lines[axis]
        for k in range(1, count):
            send(i + k, out.at[mine], out.at[mine], at(axis, lax.rem(mine + k, count)))

    def await_spread(axis, i, out):
        count, mine = lines[axis]
        for k in range(1, count):
            await_recv(i + k, out.at[lax.rem(mine - k + count, count)])

    for k in range(1, np_):
        send(Z + k, q_ref, all_ref.at[me], (lax.rem(zz + k, np_) * 2 + core, g))
    column(0)

    over_small(0, lambda cp: cp.wait())
    for i in range(n):
        nrm_f[i * sub:(i + 1) * sub] = allnrm[i].astype(f32)
    normed = nrm_f[...].astype(bf16)
    for i, (w, cp) in enumerate(((gate, local[0]), (up, local[1]))):
        cp.wait()
        part = lax.dot_general(normed, w[...], contract_last, preferred_element_type=f32).astype(bf16)
        for j in range(ng):
            gu_x[j, i * per:(i + 1) * per] = part[j * per:(j + 1) * per]
    scatter("grp", G1, gu_x, gu_buf)
    advance(1)

    over_small(1, lambda cp: cp.wait())
    over_small(2, lambda cp: cp.wait())
    for i in range(n):
        rows_f[i * sub:(i + 1) * sub] = allsub[i].astype(f32)
    sub_q = rows_f[...].astype(bf16)
    local[2].wait()
    count = docs.shape[0]
    tile = 256 if count % 256 == 0 else count

    def score(i, c):
        at_rows = pl.ds(pl.multiple_of(i * tile, tile), tile)
        scores[at_rows] = sharpness_scale * lax.dot_general(
            docs[at_rows], sub_q, contract_last, preferred_element_type=f32)
        return c

    lax.fori_loop(0, count // tile, score, 0)
    sc = scores[...]
    top = jnp.max(sc, axis=0, keepdims=True)
    st_buf[b] = jnp.zeros(st_buf.shape[1:], f32)
    st_buf[b, 0:1] = top
    st_buf[b, 1:2] = jnp.sum(jnp.exp(sc - top), axis=0, keepdims=True)
    spread("blk", S1, st_buf)
    gu_out[g] = collect("grp", G1, gu_x, gu_buf).astype(bf16)
    spread("grp", G2, gu_out)
    await_spread("blk", S1, st_buf)
    high = st_buf[0, 0:1]
    for k in range(1, nb):
        high = jnp.maximum(high, st_buf[k, 0:1])
    total = jnp.zeros_like(high)
    for k in range(nb):
        total = total + st_buf[k, 1:2] * jnp.exp(st_buf[k, 0:1] - high)
    log_total = high + jnp.log(total)
    where = allspos[0]
    for k in range(1, n):
        where = where + allspos[k]
    ids = lax.broadcasted_iota(jnp.int32, sc.shape, 0) + b * count
    weights = (jnp.exp(sc - log_total) - (ids == where[:, :sub_all]).astype(f32)).astype(bf16)
    doc_part = docs[:, pl.ds(pl.multiple_of(g * feat, 128), feat)]
    part = sharpness_scale * lax.dot_general(
        weights, doc_part, (((0,), (0,)), ((), ())), preferred_element_type=f32)
    for p in range(nb):
        cot_x[p] = part[p * block:(p + 1) * block].astype(bf16)
    scatter("blk", C1, cot_x, cot_buf)
    advance(2)
    mine = collect("blk", C1, cot_x, cot_buf).astype(bf16)
    cot_out[b] = mine
    spread("blk", C2, cot_out)
    mine_f = mine.astype(f32)
    for j in range(ng):
        cpiece[j] = mine_f[j * sub:(j + 1) * sub]
    for k in range(1, ng):
        p = lax.rem(g + k, ng)
        send(F3 + k, cpiece.at[p], cots_ref.at[g], (b, p))
    await_spread("blk", C2, cot_out)
    for p in range(nb):
        cot_f[p * block:(p + 1) * block] = cot_out[p].astype(f32)
    local[3].wait()
    part = lax.dot_general(cot_f[...].astype(bf16), down[...], contract_last, preferred_element_type=f32)
    for j in range(ng):
        act_x[j] = part[j * per:(j + 1) * per].astype(bf16)
    scatter("grp", A1, act_x, act_buf)
    act_out[g] = collect("grp", A1, act_x, act_buf).astype(bf16)
    spread("grp", A2, act_out)
    advance(2)
    await_spread("grp", G2, gu_out)
    await_spread("grp", A2, act_out)
    for j in range(ng):
        u_grad, g_grad = swiglu_grads(
            act_out[j].astype(f32), gu_out[j, 0:per].astype(f32), gu_out[j, per:2 * per].astype(f32))
        gg[j * per:(j + 1) * per] = g_grad
        ug[j * per:(j + 1) * per] = u_grad
    part = jnp.dot(gg[...], gate[...], preferred_element_type=f32)
    part = part + jnp.dot(ug[...], up[...], preferred_element_type=f32)
    for p in range(nb):
        fin_x[p] = part[p * block:(p + 1) * block].astype(bf16)
    scatter("blk", F1, fin_x, fin_buf)
    advance(2)
    done = collect("blk", F1, fin_x, fin_buf)
    for j in range(ng):
        piece[j] = done[j * sub:(j + 1) * sub]
    for k in range(1, ng):
        p = lax.rem(g + k, ng)
        send(F2 + k, piece.at[p], grad_ref.at[g], (b, p))
    grad_ref[g] = piece[g]
    cots_ref[g] = cpiece[g]
    advance(len(bulk))
    oc = 1 - core
    for k in range(np_):
        for start, gx in ((P0, g), (P1, g ^ 1), (P2, g ^ 2), (P3, g ^ 3)):
            await_recv(start + k, all_ref.at[slot(k, gx, oc)])
    await_spread("grp", F2, grad_ref)
    await_spread("grp", F3, cots_ref)
    own.wait()
    over_small(3, lambda cp: cp.wait())
    for cp in started:
        cp.wait_send()


def run_main(nb, ng, queries, pos, normed, spos, docs, gate, up, down):
    n, np_ = nb * ng, nb // 2
    sub = normed.shape[1]
    hidden, feat = gate.shape
    sub_all, block = sub * n, sub * ng
    per = sub_all // ng
    sems = 12 * np_ + 6 * ng + 4 * nb
    V = pltpu.VMEM
    any_ = pl.BlockSpec(memory_space=pl.ANY)
    return pl.pallas_call(
        functools.partial(main_kernel, nb, ng),
        out_shape=(
            jax.ShapeDtypeStruct((n,) + queries.shape, queries.dtype),
            jax.ShapeDtypeStruct((n,) + pos.shape, pos.dtype),
            jax.ShapeDtypeStruct((ng, sub, feat), f32),
            jax.ShapeDtypeStruct((ng, sub, feat), f32),
        ),
        in_specs=[VM] * 4 + [any_] * 4,
        out_specs=(any_, VM, VM, VM),
        scratch_shapes=[
            V((n, sub, feat), bf16), V((n, sub, queries.shape[1]), bf16), V((n,) + spos.shape, jnp.int32),
            V(docs.shape, bf16), V(gate.shape, bf16), V(up.shape, bf16), V(down.shape, bf16),
            V((sub_all, queries.shape[1]), f32), V((sub_all, feat), f32),
            V((ng, 2 * per, hidden), bf16), V((ng, 2 * per, hidden), bf16), V((ng, 2 * per, hidden), bf16),
            V((nb, 8, sub_all), f32),
            V((nb, block, feat), bf16), V((nb, block, feat), bf16), V((nb, block, feat), bf16),
            V((sub_all, feat), f32),
            V((ng, per, hidden), bf16), V((ng, per, hidden), bf16), V((ng, per, hidden), bf16),
            V((sub_all, hidden), bf16), V((sub_all, hidden), bf16),
            V((nb, block, feat), bf16), V((nb, block, feat), bf16),
            V((ng, sub, feat), f32), V((ng, sub, feat), f32),
            V((docs.shape[0], sub_all), f32),
            V((sub, queries.shape[1]), bf16),
            DMA((5,)), DMA((sems,)), DMA((sems,)), DMA((4, n)), DMA((4, n)),
        ],
        compiler_params=params(0),
    )(queries, pos, normed, spos, docs, gate, up, down)


def peer(axis, b, g, p):
    return (p, g) if axis == "blk" else (b, p)


def greet_axes(nb, ng, axes):
    b, g = lax.axis_index("blk"), lax.axis_index("grp")
    barrier = pltpu.get_barrier_semaphore()
    total = 0
    for axis, n, me in (("blk", nb, b), ("grp", ng, g)):
        if axis in axes:
            for k in range(1, n):
                pl.semaphore_signal(barrier, inc=1, device_id=peer(axis, b, g, lax.rem(me + k, n)),
                                    device_id_type=MESH)
            total += n - 1
    pl.semaphore_wait(barrier, total)
    return b, g


def combine(buf, n):
    top = buf[0, 0]
    for k in range(1, n):
        top = jnp.maximum(top, buf[k, 0])
    total, hit = jnp.zeros_like(top), jnp.zeros_like(top)
    for k in range(n):
        total = total + buf[k, 1] * jnp.exp(buf[k, 0] - top)
        hit = hit + buf[k, 2]
    return top, total, hit


def stats_kernel(nb, ng, x_ref, out_ref, buf1, buf2, s1, r1, s2, r2):
    b, g = greet_axes(nb, ng, ("blk", "grp"))
    copies = []
    for k in range(1, ng):
        cp = remote(x_ref, buf1.at[g], s1.at[k], r1.at[k], (b, lax.rem(g + k, ng)))
        cp.start()
        copies.append(cp)
    buf1[g] = x_ref[...]
    for cp in copies:
        cp.wait()
    for i, v in enumerate(combine(buf1, ng)):
        buf2[b, i] = v
    copies = []
    for k in range(1, nb):
        cp = remote(buf2.at[b], buf2.at[b], s2.at[k], r2.at[k], (lax.rem(b + k, nb), g))
        cp.start()
        copies.append(cp)
    for cp in copies:
        cp.wait()
    top, total, hit = combine(buf2, nb)
    out_ref[0] = top + jnp.log(total)
    out_ref[1] = hit


def share_stats(nb, ng, x):
    return pl.pallas_call(
        functools.partial(stats_kernel, nb, ng),
        out_shape=jax.ShapeDtypeStruct((2,) + x.shape[1:], f32),
        in_specs=[VM],
        out_specs=VM,
        scratch_shapes=[pltpu.VMEM((ng,) + x.shape, f32), pltpu.VMEM((nb,) + x.shape, f32),
                        DMA((ng,)), DMA((ng,)), DMA((nb,)), DMA((nb,))],
        compiler_params=params(2),
    )(x)


def row_norm(hidden):
    hidden_f = hidden.astype(f32)
    inv_rms = lax.rsqrt(jnp.mean(hidden_f * hidden_f, axis=1, keepdims=True) + epsilon)
    return (hidden_f, inv_rms)


def swiglu_grads(act_grad, gate_value, up_value):
    gate_sigmoid = jax.nn.sigmoid(gate_value)
    up_grad = (act_grad * gate_value * gate_sigmoid).astype(bf16)
    gate_grad = (
        act_grad * up_value * gate_sigmoid * (1.0 + gate_value * (1.0 - gate_sigmoid))
    ).astype(bf16)
    return (up_grad, gate_grad)


def shards(nb, ng, queries, docs, positive, last_hidden, norm_gain, gate_weight, up_weight, down_weight):
    b, g = lax.axis_index("blk"), lax.axis_index("grp")
    n, (rows, width) = nb * ng, queries.shape
    total_rows = n * rows
    sub = last_hidden.shape[0]
    sub_all = sub * n
    feat = gate_weight.shape[0]
    shard_rows = docs.shape[0]
    own_docs = shard_rows // ng

    hidden_f, inv_rms = row_norm(last_hidden)
    normed = (hidden_f * inv_rms * norm_gain).astype(bf16)
    normed = normed.reshape(sub, ng, feat).transpose(1, 0, 2)
    pos = jnp.pad(positive.reshape(1, rows), ((0, 0), (0, 128 - rows)))
    lanes = -(-sub_all // 128) * 128
    spos = lax.dynamic_update_slice(
        jnp.zeros((1, lanes), jnp.int32), positive[:sub].reshape(1, sub), (0, (b * ng + g) * sub))
    all_q, all_pos, normed_grad, cots = run_main(
        nb, ng, queries, pos, normed, spos, docs, gate_weight.T, up_weight.T, down_weight)
    q = all_q.reshape(total_rows, width)
    pos = all_pos[:, 0, :rows].reshape(total_rows)

    mine = lax.dynamic_slice_in_dim(docs, g * own_docs, own_docs)
    scores = sharpness_scale * lax.dot_general(mine, q, contract_last, preferred_element_type=f32)
    ids = lax.broadcasted_iota(jnp.int32, (own_docs, 1), 0) + (b * shard_rows + g * own_docs)
    hits = ids == pos[None, :]
    top = jnp.max(scores, axis=0)
    summed = jnp.sum(jnp.exp(scores - top[None, :]), axis=0)
    hit = jnp.sum(jnp.where(hits, scores, 0.0), axis=0)
    stats = jnp.stack([top, summed, hit]).reshape(3, total_rows // 128, 128)
    done = share_stats(nb, ng, stats).reshape(2, total_rows)
    log_total, pos_logit = done[0], done[1]
    losses = lax.dynamic_slice_in_dim(log_total - pos_logit, (b * ng + g) * rows, rows)
    weights = (jnp.exp(scores - log_total[None, :]) - hits.astype(f32)).astype(bf16)
    passage_grads = sharpness_scale * jnp.dot(weights, q, preferred_element_type=f32)

    normed_grad = normed_grad.transpose(1, 0, 2).reshape(sub, width)
    cots = cots.transpose(1, 0, 2).reshape(sub, width)
    scaled = normed_grad * norm_gain
    hidden_grads = (
        cots
        + inv_rms * scaled
        - hidden_f
        * inv_rms
        * inv_rms
        * inv_rms
        * jnp.mean(hidden_f * scaled, axis=1, keepdims=True)
    )
    return (losses, passage_grads, hidden_grads)


def solution(mesh):
    return jax.shard_map(
        functools.partial(shards, mesh.shape["blk"], mesh.shape["grp"]),
        mesh=mesh,
        in_specs=(
            P(("blk", "grp"), None),
            P("blk", None),
            P(("blk", "grp")),
            P(("blk", "grp"), None),
            P(),
            P("grp", "blk"),
            P("grp", "blk"),
            P("blk", "grp"),
        ),
        out_specs=(P(("blk", "grp")), P(("blk", "grp"), None), P(("blk", "grp"), None)),
        check_vma=False,
    )
```

```python
import functools

import jax
import jax.numpy as jnp
from jax import lax
from jax.experimental import pallas as pl
from jax.experimental.pallas import tpu as pltpu
from jax.sharding import PartitionSpec as P

sharpness_scale = 20.0
epsilon = 1e-06
contract_last = (((1,), (1,)), ((), ()))
MESH = pl.DeviceIdType.MESH
VM = pl.BlockSpec(memory_space=pltpu.VMEM)
DMA = pltpu.SemaphoreType.DMA
f32, bf16 = jnp.float32, jnp.bfloat16


def remote(src, dst, ssem, rsem, dev):
    return pltpu.make_async_remote_copy(
        src_ref=src, dst_ref=dst, send_sem=ssem, recv_sem=rsem, device_id=dev, device_id_type=MESH
    )


def params(cid):
    return pltpu.CompilerParams(collective_id=cid, has_side_effects=True)


def main_kernel(nb, ng, q_ref, pos_ref, nrm_ref, spos_ref, docs_hbm, gate_hbm, up_hbm, down_hbm,
                all_ref, allpos_ref, grad_ref, cots_ref, score_ref, stat_ref,
                allnrm, allsub, allspos, docs, gate, up, down, rows_f, nrm_f,
                gu_x, gu_buf, gu_out, st_buf, cot_x, cot_buf, cot_out, cot_f, act_x, act_buf, act_out,
                gg, ug, fin_x, fin_buf, piece, cpiece, scores,
                subq_ref, qbuf, posrow, t1, t2, loc_sem, ssem, rsem, small_s, small_r):
    b, g = lax.axis_index("blk"), lax.axis_index("grp")
    n, me = nb * ng, b * ng + g
    np_, zz, core = nb // 2, b // 2, b % 2
    half = q_ref.shape[0] // 2
    sub = subq_ref.shape[0]
    sub_all, feat, block = sub * n, gate.shape[1], sub * ng
    per = sub_all // ng
    barrier = pltpu.get_barrier_semaphore()
    subq_ref[...] = q_ref[0:sub]

    def greet(k, c):
        p = lax.rem(me + k, n)
        pl.semaphore_signal(barrier, inc=1, device_id=(p // ng, p % ng), device_id_type=MESH)
        return c

    local = []
    for i, (src, dst) in enumerate(((gate_hbm, gate), (up_hbm, up), (docs_hbm, docs), (down_hbm, down))):
        cp = pltpu.make_async_copy(src, dst, loc_sem.at[i + 1])
        cp.start()
        local.append(cp)
    lax.fori_loop(1, n, greet, 0)
    pl.semaphore_wait(barrier, n - 1)

    def small(i, k):
        p = lax.rem(me + k, n)
        src, dst = ((nrm_ref.at[p % ng], allnrm), (subq_ref, allsub),
                    (spos_ref, allspos), (pos_ref, allpos_ref), (q_ref, all_ref))[i]
        return remote(src, dst.at[me], small_s.at[i, k], small_r.at[i, k], (p // ng, p % ng))

    def over_small(which, act):
        def go(k, c):
            act(small(which, k))
            return c
        lax.fori_loop(1, n, go, 0)

    direct = ng != 4
    for i in range(5 if direct else 4):
        over_small(i, lambda cp: cp.start())
    own = pltpu.make_async_copy(q_ref, all_ref.at[me], loc_sem.at[0])
    own.start()
    allnrm[me] = nrm_ref[g]
    allsub[me] = subq_ref[...]
    allspos[me] = spos_ref[...]
    allpos_ref[me] = pos_ref[...]

    started = []

    def slot(k, gg_, cc):
        return (lax.rem(zz - k + np_, np_) * 2 + cc) * ng + gg_

    def send(i, src, dst, dev):
        cp = remote(src, dst, ssem.at[i], rsem.at[i], dev)
        cp.start()
        started.append(cp)

    def await_recv(i, region):
        remote(region, region, ssem.at[i], rsem.at[i], (b, g ^ 1)).wait_recv()

    A, B = pl.ds(0, half), pl.ds(half, half)
    Z, XA, XB, YA, YB, DA, DB, P0, P1, P2, P3, base = [i * np_ for i in range(12)]
    xdev, ydev, pdev = (b, g ^ 1), (b, g ^ 2), (b ^ 1, g)

    def column(k):
        s = slot(k, g, core)
        if k == 0:
            src, pa, pb = q_ref, q_ref.at[A], q_ref.at[B]
        else:
            await_recv(Z + k, all_ref.at[s])
            src = all_ref.at[s]
            pa, pb = all_ref.at[s, A], all_ref.at[s, B]
        send(XA + k, pa, all_ref.at[s, A], xdev)
        send(YB + k, pb, all_ref.at[s, B], ydev)
        send(XB + k, pb, all_ref.at[s, B], xdev)
        send(YA + k, pa, all_ref.at[s, A], ydev)
        send(P0 + k, src, all_ref.at[s], pdev)

    def forward(k):
        sx, sy = slot(k, g ^ 1, core), slot(k, g ^ 2, core)
        await_recv(XA + k, all_ref.at[sx, A])
        send(DA + k, all_ref.at[sx, A], all_ref.at[sx, A], ydev)
        await_recv(YB + k, all_ref.at[sy, B])
        send(DB + k, all_ref.at[sy, B], all_ref.at[sy, B], xdev)

    def share(k):
        sx, sy = slot(k, g ^ 1, core), slot(k, g ^ 2, core)
        await_recv(XB + k, all_ref.at[sx, B])
        send(P1 + k, all_ref.at[sx], all_ref.at[sx], pdev)
        await_recv(YA + k, all_ref.at[sy, A])
        send(P2 + k, all_ref.at[sy], all_ref.at[sy], pdev)

    def share_diag(k):
        sd = slot(k, g ^ 3, core)
        await_recv(DA + k, all_ref.at[sd, A])
        await_recv(DB + k, all_ref.at[sd, B])
        send(P3 + k, all_ref.at[sd], all_ref.at[sd], pdev)

    bulk = [functools.partial(column, k) for k in range(1, 2)]
    for k in range(2, np_):
        bulk += [functools.partial(column, k), functools.partial(forward, k - 2)]
    for k in range(max(np_ - 2, 0), np_):
        bulk += [functools.partial(forward, k)]
    bulk += [functools.partial(share, k) for k in range(np_)]
    bulk += [functools.partial(share_diag, k) for k in range(np_)]

    if direct:
        bulk = []

    def advance(count):
        for _ in range(min(count, len(bulk))):
            bulk.pop(0)()

    G1, G2 = base, base + ng
    A1, A2 = G2 + ng, G2 + 2 * ng
    F2, F3 = A2 + ng, A2 + 2 * ng
    S1 = F3 + ng
    C1, C2, F1 = S1 + nb, S1 + 2 * nb, S1 + 3 * nb
    T2, T1 = S1 + 4 * nb, S1 + 5 * nb
    lines = {"grp": (ng, g), "blk": (nb, b)}

    def at(axis, p):
        return (p, g) if axis == "blk" else (b, p)

    def scatter(axis, i, x, buf):
        count, mine = lines[axis]
        for k in range(1, count):
            p = lax.rem(mine + k, count)
            send(i + k, x.at[p], buf.at[k], at(axis, p))

    def collect(axis, i, x, buf):
        count, mine = lines[axis]
        acc = x[mine].astype(f32)
        for k in range(1, count):
            await_recv(i + k, buf.at[k])
            acc = acc + buf[k].astype(f32)
        return acc

    def spread(axis, i, out):
        count, mine = lines[axis]
        for k in range(1, count):
            send(i + k, out.at[mine], out.at[mine], at(axis, lax.rem(mine + k, count)))

    def await_spread(axis, i, out):
        count, mine = lines[axis]
        for k in range(1, count):
            await_recv(i + k, out.at[lax.rem(mine - k + count, count)])

    if not direct:
        for k in range(1, np_):
            send(Z + k, q_ref, all_ref.at[me], (lax.rem(zz + k, np_) * 2 + core, g))
        column(0)

    over_small(0, lambda cp: cp.wait())
    for i in range(n):
        nrm_f[i * sub:(i + 1) * sub] = allnrm[i].astype(f32)
    normed = nrm_f[...].astype(bf16)
    for i, (w, cp) in enumerate(((gate, local[0]), (up, local[1]))):
        cp.wait()
        part = lax.dot_general(normed, w[...], contract_last, preferred_element_type=f32).astype(bf16)
        for j in range(ng):
            gu_x[j, i * per:(i + 1) * per] = part[j * per:(j + 1) * per]
    scatter("grp", G1, gu_x, gu_buf)
    advance(1)

    over_small(1, lambda cp: cp.wait())
    over_small(2, lambda cp: cp.wait())
    for i in range(n):
        rows_f[i * sub:(i + 1) * sub] = allsub[i].astype(f32)
    sub_q = rows_f[...].astype(bf16)
    local[2].wait()
    count = docs.shape[0]
    tile = 256 if count % 256 == 0 else count

    def score(i, c):
        at_rows = pl.ds(pl.multiple_of(i * tile, tile), tile)
        scores[at_rows] = sharpness_scale * lax.dot_general(
            docs[at_rows], sub_q, contract_last, preferred_element_type=f32)
        return c

    lax.fori_loop(0, count // tile, score, 0)
    sc = scores[...]
    top = jnp.max(sc, axis=0, keepdims=True)
    st_buf[b] = jnp.zeros(st_buf.shape[1:], f32)
    st_buf[b, 0:1] = top
    st_buf[b, 1:2] = jnp.sum(jnp.exp(sc - top), axis=0, keepdims=True)
    spread("blk", S1, st_buf)
    gu_out[g] = collect("grp", G1, gu_x, gu_buf).astype(bf16)
    spread("grp", G2, gu_out)
    await_spread("blk", S1, st_buf)
    high = st_buf[0, 0:1]
    for k in range(1, nb):
        high = jnp.maximum(high, st_buf[k, 0:1])
    total = jnp.zeros_like(high)
    for k in range(nb):
        total = total + st_buf[k, 1:2] * jnp.exp(st_buf[k, 0:1] - high)
    log_total = high + jnp.log(total)
    where = allspos[0]
    for k in range(1, n):
        where = where + allspos[k]
    ids = lax.broadcasted_iota(jnp.int32, sc.shape, 0) + b * count
    weights = (jnp.exp(sc - log_total) - (ids == where[:, :sub_all]).astype(f32)).astype(bf16)
    if feat % 128 == 0:
        doc_part = docs[:, pl.ds(pl.multiple_of(g * feat, 128), feat)]
    else:
        doc_part = docs[:, 0:feat]
        for j in range(1, ng):
            doc_part = jnp.where(g == j, docs[:, j * feat:(j + 1) * feat], doc_part)
    part = sharpness_scale * lax.dot_general(
        weights, doc_part, (((0,), (0,)), ((), ())), preferred_element_type=f32)
    for p in range(nb):
        cot_x[p] = part[p * block:(p + 1) * block].astype(bf16)
    scatter("blk", C1, cot_x, cot_buf)
    advance(2)
    mine = collect("blk", C1, cot_x, cot_buf).astype(bf16)
    cot_out[b] = mine
    spread("blk", C2, cot_out)
    mine_f = mine.astype(f32)
    for j in range(ng):
        cpiece[j] = mine_f[j * sub:(j + 1) * sub]
    for k in range(1, ng):
        p = lax.rem(g + k, ng)
        send(F3 + k, cpiece.at[p], cots_ref.at[g], (b, p))
    await_spread("blk", C2, cot_out)
    for p in range(nb):
        cot_f[p * block:(p + 1) * block] = cot_out[p].astype(f32)
    local[3].wait()
    part = lax.dot_general(cot_f[...].astype(bf16), down[...], contract_last, preferred_element_type=f32)
    for j in range(ng):
        act_x[j] = part[j * per:(j + 1) * per].astype(bf16)
    scatter("grp", A1, act_x, act_buf)
    act_out[g] = collect("grp", A1, act_x, act_buf).astype(bf16)
    spread("grp", A2, act_out)
    advance(2)
    await_spread("grp", G2, gu_out)
    await_spread("grp", A2, act_out)
    for j in range(ng):
        u_grad, g_grad = swiglu_grads(
            act_out[j].astype(f32), gu_out[j, 0:per].astype(f32), gu_out[j, per:2 * per].astype(f32))
        gg[j * per:(j + 1) * per] = g_grad
        ug[j * per:(j + 1) * per] = u_grad
    part = jnp.dot(gg[...], gate[...], preferred_element_type=f32)
    part = part + jnp.dot(ug[...], up[...], preferred_element_type=f32)
    for p in range(nb):
        fin_x[p] = part[p * block:(p + 1) * block].astype(bf16)
    scatter("blk", F1, fin_x, fin_buf)
    advance(len(bulk))
    oc = 1 - core
    if direct:
        over_small(4, lambda cp: cp.wait())
    for k in range(0 if direct else np_):
        for start, gx in ((P0, g), (P1, g ^ 1), (P2, g ^ 2), (P3, g ^ 3)):
            await_recv(start + k, all_ref.at[slot(k, gx, oc)])
    own.wait()
    over_small(3, lambda cp: cp.wait())
    r, own_docs, slots = q_ref.shape[0], score_ref.shape[0], qbuf.shape[1]
    wide = slots * r
    for i in range(n):
        posrow[:, i * r:(i + 1) * r] = allpos_ref[i][:, 0:r]

    def fetch(c):
        return pltpu.make_async_copy(
            all_ref.at[pl.ds(c * slots, slots)], qbuf.at[c % 2], loc_sem.at[5 + c % 2])

    fetch(0).start()
    mine_docs = docs[pl.ds(pl.multiple_of(g * own_docs, own_docs), own_docs)]
    ids = lax.broadcasted_iota(jnp.int32, (own_docs, wide), 0) + (b * count + g * own_docs)
    t1[g] = jnp.zeros(t1.shape[1:], f32)
    for c in range(n // slots):
        if c + 1 < n // slots:
            fetch(c + 1).start()
        fetch(c).wait()
        cols = slice(c * wide, (c + 1) * wide)
        sc = sharpness_scale * lax.dot_general(
            mine_docs, qbuf[c % 2].reshape(wide, q_ref.shape[1]), contract_last, preferred_element_type=f32)
        score_ref[:, cols] = sc
        top = jnp.max(sc, axis=0, keepdims=True)
        t1[g, 0:1, cols] = top
        t1[g, 1:2, cols] = jnp.sum(jnp.exp(sc - top), axis=0, keepdims=True)
        t1[g, 2:3, cols] = jnp.sum(jnp.where(ids == posrow[:, cols], sc, 0.0), axis=0, keepdims=True)
    spread("grp", T1, t1)
    done = collect("blk", F1, fin_x, fin_buf)
    for j in range(ng):
        piece[j] = done[j * sub:(j + 1) * sub]
    for k in range(1, ng):
        p = lax.rem(g + k, ng)
        send(F2 + k, piece.at[p], grad_ref.at[g], (b, p))
    grad_ref[g] = piece[g]
    cots_ref[g] = cpiece[g]

    def merge(buf, length):
        high = buf[0, 0:1]
        for k in range(1, length):
            high = jnp.maximum(high, buf[k, 0:1])
        total, hit = jnp.zeros_like(high), jnp.zeros_like(high)
        for k in range(length):
            total = total + buf[k, 1:2] * jnp.exp(buf[k, 0:1] - high)
            hit = hit + buf[k, 2:3]
        return high, total, hit

    await_spread("grp", T1, t1)
    t2[b] = jnp.zeros(t2.shape[1:], f32)
    for i, v in enumerate(merge(t1, ng)):
        t2[b, i:i + 1] = v
    spread("blk", T2, t2)
    await_spread("blk", T2, t2)
    high, total, hit = merge(t2, nb)
    stat_ref[0:1] = high + jnp.log(total)
    stat_ref[1:2] = hit
    await_spread("grp", F2, grad_ref)
    await_spread("grp", F3, cots_ref)
    for cp in started:
        cp.wait_send()


def run_main(nb, ng, queries, pos, normed, spos, docs, gate, up, down):
    n, np_ = nb * ng, nb // 2
    sub = normed.shape[1]
    hidden, feat = gate.shape
    sub_all, block = sub * n, sub * ng
    per = sub_all // ng
    sems = 12 * np_ + 7 * ng + 5 * nb
    total = n * queries.shape[0]
    slots = max(1, 256 // queries.shape[0])
    own_docs = docs.shape[0] // ng
    V = pltpu.VMEM
    any_ = pl.BlockSpec(memory_space=pl.ANY)
    return pl.pallas_call(
        functools.partial(main_kernel, nb, ng),
        out_shape=(
            jax.ShapeDtypeStruct((n,) + queries.shape, queries.dtype),
            jax.ShapeDtypeStruct((n,) + pos.shape, pos.dtype),
            jax.ShapeDtypeStruct((ng, sub, feat), f32),
            jax.ShapeDtypeStruct((ng, sub, feat), f32),
            jax.ShapeDtypeStruct((own_docs, total), f32),
            jax.ShapeDtypeStruct((2, total), f32),
        ),
        in_specs=[VM] * 4 + [any_] * 4,
        out_specs=(any_, VM, VM, VM, VM, VM),
        scratch_shapes=[
            V((n, sub, feat), bf16), V((n, sub, queries.shape[1]), bf16), V((n,) + spos.shape, jnp.int32),
            V(docs.shape, bf16), V(gate.shape, bf16), V(up.shape, bf16), V(down.shape, bf16),
            V((sub_all, queries.shape[1]), f32), V((sub_all, feat), f32),
            V((ng, 2 * per, hidden), bf16), V((ng, 2 * per, hidden), bf16), V((ng, 2 * per, hidden), bf16),
            V((nb, 8, sub_all), f32),
            V((nb, block, feat), bf16), V((nb, block, feat), bf16), V((nb, block, feat), bf16),
            V((sub_all, feat), f32),
            V((ng, per, hidden), bf16), V((ng, per, hidden), bf16), V((ng, per, hidden), bf16),
            V((sub_all, hidden), bf16), V((sub_all, hidden), bf16),
            V((nb, block, feat), bf16), V((nb, block, feat), bf16),
            V((ng, sub, feat), f32), V((ng, sub, feat), f32),
            V((docs.shape[0], sub_all), f32),
            V((sub, queries.shape[1]), bf16),
            V((2, slots) + queries.shape, bf16), V((1, total), jnp.int32),
            V((ng, 4, total), f32), V((nb, 4, total), f32),
            DMA((7,)), DMA((sems,)), DMA((sems,)), DMA((5, n)), DMA((5, n)),
        ],
        compiler_params=params(0),
    )(queries, pos, normed, spos, docs, gate, up, down)


def row_norm(hidden):
    hidden_f = hidden.astype(f32)
    inv_rms = lax.rsqrt(jnp.mean(hidden_f * hidden_f, axis=1, keepdims=True) + epsilon)
    return (hidden_f, inv_rms)


def swiglu_grads(act_grad, gate_value, up_value):
    gate_sigmoid = jax.nn.sigmoid(gate_value)
    up_grad = (act_grad * gate_value * gate_sigmoid).astype(bf16)
    gate_grad = (
        act_grad * up_value * gate_sigmoid * (1.0 + gate_value * (1.0 - gate_sigmoid))
    ).astype(bf16)
    return (up_grad, gate_grad)


def shards(nb, ng, queries, docs, positive, last_hidden, norm_gain, gate_weight, up_weight, down_weight):
    b, g = lax.axis_index("blk"), lax.axis_index("grp")
    n, (rows, width) = nb * ng, queries.shape
    total_rows = n * rows
    sub = last_hidden.shape[0]
    sub_all = sub * n
    feat = gate_weight.shape[0]
    shard_rows = docs.shape[0]
    own_docs = shard_rows // ng

    hidden_f, inv_rms = row_norm(last_hidden)
    normed = (hidden_f * inv_rms * norm_gain).astype(bf16)
    normed = normed.reshape(sub, ng, feat).transpose(1, 0, 2)
    pos = jnp.pad(positive.reshape(1, rows), ((0, 0), (0, 128 - rows)))
    lanes = -(-sub_all // 128) * 128
    spos = lax.dynamic_update_slice(
        jnp.zeros((1, lanes), jnp.int32), positive[:sub].reshape(1, sub), (0, (b * ng + g) * sub))
    all_q, all_pos, normed_grad, cots, scores, done = run_main(
        nb, ng, queries, pos, normed, spos, docs, gate_weight.T, up_weight.T, down_weight)
    q = all_q.reshape(total_rows, width)
    pos = all_pos[:, 0, :rows].reshape(total_rows)

    ids = lax.broadcasted_iota(jnp.int32, (own_docs, 1), 0) + (b * shard_rows + g * own_docs)
    hits = ids == pos[None, :]
    log_total, pos_logit = done[0], done[1]
    losses = lax.dynamic_slice_in_dim(log_total - pos_logit, (b * ng + g) * rows, rows)
    weights = (jnp.exp(scores - log_total[None, :]) - hits.astype(f32)).astype(bf16)
    passage_grads = sharpness_scale * jnp.dot(weights, q, preferred_element_type=f32)

    normed_grad = normed_grad.transpose(1, 0, 2).reshape(sub, width)
    cots = cots.transpose(1, 0, 2).reshape(sub, width)
    scaled = normed_grad * norm_gain
    hidden_grads = (
        cots
        + inv_rms * scaled
        - hidden_f
        * inv_rms
        * inv_rms
        * inv_rms
        * jnp.mean(hidden_f * scaled, axis=1, keepdims=True)
    )
    return (losses, passage_grads, hidden_grads)


def solution(mesh):
    return jax.shard_map(
        functools.partial(shards, mesh.shape["blk"], mesh.shape["grp"]),
        mesh=mesh,
        in_specs=(
            P(("blk", "grp"), None),
            P("blk", None),
            P(("blk", "grp")),
            P(("blk", "grp"), None),
            P(),
            P("grp", "blk"),
            P("grp", "blk"),
            P("blk", "grp"),
        ),
        out_specs=(P(("blk", "grp")), P(("blk", "grp"), None), P(("blk", "grp"), None)),
        check_vma=False,
    )
```

```python
import functools

import jax
import jax.numpy as jnp
from jax import lax
from jax.experimental import pallas as pl
from jax.experimental.pallas import tpu as pltpu
from jax.sharding import PartitionSpec as P

sharpness_scale = 20.0
epsilon = 1e-06
contract_last = (((1,), (1,)), ((), ()))
MESH = pl.DeviceIdType.MESH
VM = pl.BlockSpec(memory_space=pltpu.VMEM)
DMA = pltpu.SemaphoreType.DMA
f32, bf16 = jnp.float32, jnp.bfloat16


def remote(src, dst, ssem, rsem, dev):
    return pltpu.make_async_remote_copy(
        src_ref=src, dst_ref=dst, send_sem=ssem, recv_sem=rsem, device_id=dev, device_id_type=MESH
    )


def params(cid):
    return pltpu.CompilerParams(collective_id=cid, has_side_effects=True)


def main_kernel(nb, ng, q_ref, pos_ref, nrm_ref, spos_ref, docs_hbm, gate_hbm, up_hbm, down_hbm,
                all_ref, allpos_ref, grad_ref, cots_ref, score_ref, stat_ref,
                allnrm, allsub, allspos, docs, gate, up, down, rows_f, nrm_f,
                gu_x, gu_buf, gu_out, st_buf, cot_x, cot_buf, cot_out, cot_f, act_x, act_buf, act_out,
                gg, ug, fin_x, fin_buf, piece, cpiece, scores,
                subq_ref, qbuf, posrow, t1, t2, loc_sem, ssem, rsem, small_s, small_r):
    b, g = lax.axis_index("blk"), lax.axis_index("grp")
    n, me = nb * ng, b * ng + g
    np_, zz, core = nb // 2, b // 2, b % 2
    half = q_ref.shape[0] // 2
    sub = subq_ref.shape[0]
    sub_all, feat, block = sub * n, gate.shape[1], sub * ng
    per = sub_all // ng
    barrier = pltpu.get_barrier_semaphore()
    subq_ref[...] = q_ref[0:sub]

    def greet(k, c):
        p = lax.rem(me + k, n)
        pl.semaphore_signal(barrier, inc=1, device_id=(p // ng, p % ng), device_id_type=MESH)
        return c

    local = []
    for i, (src, dst) in enumerate(((gate_hbm, gate), (up_hbm, up), (docs_hbm, docs), (down_hbm, down))):
        cp = pltpu.make_async_copy(src, dst, loc_sem.at[i + 1])
        cp.start()
        local.append(cp)
    lax.fori_loop(1, n, greet, 0)
    pl.semaphore_wait(barrier, n - 1)

    def small(i, k):
        p = lax.rem(me + k, n)
        src, dst = ((nrm_ref.at[p % ng], allnrm), (subq_ref, allsub),
                    (spos_ref, allspos), (pos_ref, allpos_ref), (q_ref, all_ref))[i]
        return remote(src, dst.at[me], small_s.at[i, k], small_r.at[i, k], (p // ng, p % ng))

    def over_small(which, act):
        def go(k, c):
            act(small(which, k))
            return c
        lax.fori_loop(1, n, go, 0)

    direct = ng != 4
    for i in range(5 if direct else 4):
        over_small(i, lambda cp: cp.start())
    own = pltpu.make_async_copy(q_ref, all_ref.at[me], loc_sem.at[0])
    own.start()
    allnrm[me] = nrm_ref[g]
    allsub[me] = subq_ref[...]
    allspos[me] = spos_ref[...]
    allpos_ref[me] = pos_ref[...]

    started = []

    def slot(k, gg_, cc):
        return (lax.rem(zz - k + np_, np_) * 2 + cc) * ng + gg_

    def send(i, src, dst, dev):
        cp = remote(src, dst, ssem.at[i], rsem.at[i], dev)
        cp.start()
        started.append(cp)

    def await_recv(i, region):
        remote(region, region, ssem.at[i], rsem.at[i], (b, g ^ 1)).wait_recv()

    A, B = pl.ds(0, half), pl.ds(half, half)
    Z, XA, XB, YA, YB, DA, DB, P0, P1, P2, P3, base = [i * np_ for i in range(12)]
    xdev, ydev, pdev = (b, g ^ 1), (b, g ^ 2), (b ^ 1, g)

    def column(k):
        s = slot(k, g, core)
        if k == 0:
            src, pa, pb = q_ref, q_ref.at[A], q_ref.at[B]
        else:
            await_recv(Z + k, all_ref.at[s])
            src = all_ref.at[s]
            pa, pb = all_ref.at[s, A], all_ref.at[s, B]
        send(XA + k, pa, all_ref.at[s, A], xdev)
        send(YB + k, pb, all_ref.at[s, B], ydev)
        send(XB + k, pb, all_ref.at[s, B], xdev)
        send(YA + k, pa, all_ref.at[s, A], ydev)
        send(P0 + k, src, all_ref.at[s], pdev)

    def forward(k):
        sx, sy = slot(k, g ^ 1, core), slot(k, g ^ 2, core)
        await_recv(XA + k, all_ref.at[sx, A])
        send(DA + k, all_ref.at[sx, A], all_ref.at[sx, A], ydev)
        await_recv(YB + k, all_ref.at[sy, B])
        send(DB + k, all_ref.at[sy, B], all_ref.at[sy, B], xdev)

    def share(k):
        sx, sy = slot(k, g ^ 1, core), slot(k, g ^ 2, core)
        await_recv(XB + k, all_ref.at[sx, B])
        send(P1 + k, all_ref.at[sx], all_ref.at[sx], pdev)
        await_recv(YA + k, all_ref.at[sy, A])
        send(P2 + k, all_ref.at[sy], all_ref.at[sy], pdev)

    def share_diag(k):
        sd = slot(k, g ^ 3, core)
        await_recv(DA + k, all_ref.at[sd, A])
        await_recv(DB + k, all_ref.at[sd, B])
        send(P3 + k, all_ref.at[sd], all_ref.at[sd], pdev)

    bulk = [functools.partial(column, k) for k in range(1, 2)]
    for k in range(2, np_):
        bulk += [functools.partial(column, k), functools.partial(forward, k - 2)]
    for k in range(max(np_ - 2, 0), np_):
        bulk += [functools.partial(forward, k)]
    bulk += [functools.partial(share, k) for k in range(np_)]
    bulk += [functools.partial(share_diag, k) for k in range(np_)]

    if direct:
        bulk = []

    def advance(count):
        for _ in range(min(count, len(bulk))):
            bulk.pop(0)()

    G1, G2 = base, base + ng
    A1, A2 = G2 + ng, G2 + 2 * ng
    F2, F3 = A2 + ng, A2 + 2 * ng
    S1 = F3 + ng
    C1, C2, F1 = S1 + nb, S1 + 2 * nb, S1 + 3 * nb
    T2, T1 = S1 + 4 * nb, S1 + 5 * nb
    lines = {"grp": (ng, g), "blk": (nb, b)}

    def at(axis, p):
        return (p, g) if axis == "blk" else (b, p)

    def scatter(axis, i, x, buf):
        count, mine = lines[axis]
        for k in range(1, count):
            p = lax.rem(mine + k, count)
            send(i + k, x.at[p], buf.at[k], at(axis, p))

    def collect(axis, i, x, buf):
        count, mine = lines[axis]
        acc = x[mine].astype(f32)
        for k in range(1, count):
            await_recv(i + k, buf.at[k])
            acc = acc + buf[k].astype(f32)
        return acc

    def spread(axis, i, out):
        count, mine = lines[axis]
        for k in range(1, count):
            send(i + k, out.at[mine], out.at[mine], at(axis, lax.rem(mine + k, count)))

    def await_spread(axis, i, out):
        count, mine = lines[axis]
        for k in range(1, count):
            await_recv(i + k, out.at[lax.rem(mine - k + count, count)])

    if not direct:
        for k in range(1, np_):
            send(Z + k, q_ref, all_ref.at[me], (lax.rem(zz + k, np_) * 2 + core, g))
        column(0)

    over_small(0, lambda cp: cp.wait())
    for i in range(n):
        nrm_f[i * sub:(i + 1) * sub] = allnrm[i].astype(f32)
    normed = nrm_f[...].astype(bf16)
    for i, (w, cp) in enumerate(((gate, local[0]), (up, local[1]))):
        cp.wait()
        part = lax.dot_general(normed, w[...], contract_last, preferred_element_type=f32).astype(bf16)
        for j in range(ng):
            gu_x[j, i * per:(i + 1) * per] = part[j * per:(j + 1) * per]
    scatter("grp", G1, gu_x, gu_buf)
    advance(1)

    over_small(1, lambda cp: cp.wait())
    over_small(2, lambda cp: cp.wait())
    for i in range(n):
        rows_f[i * sub:(i + 1) * sub] = allsub[i].astype(f32)
    sub_q = rows_f[...].astype(bf16)
    local[2].wait()
    count = docs.shape[0]
    tile = 256 if count % 256 == 0 else count

    def score(i, c):
        at_rows = pl.ds(pl.multiple_of(i * tile, tile), tile)
        scores[at_rows] = sharpness_scale * lax.dot_general(
            docs[at_rows], sub_q, contract_last, preferred_element_type=f32)
        return c

    lax.fori_loop(0, count // tile, score, 0)
    sc = scores[...]
    top = jnp.max(sc, axis=0, keepdims=True)
    st_buf[b] = jnp.zeros(st_buf.shape[1:], f32)
    st_buf[b, 0:1] = top
    st_buf[b, 1:2] = jnp.sum(jnp.exp(sc - top), axis=0, keepdims=True)
    spread("blk", S1, st_buf)
    advance(2)
    gu_out[g] = collect("grp", G1, gu_x, gu_buf).astype(bf16)
    spread("grp", G2, gu_out)
    await_spread("blk", S1, st_buf)
    high = st_buf[0, 0:1]
    for k in range(1, nb):
        high = jnp.maximum(high, st_buf[k, 0:1])
    total = jnp.zeros_like(high)
    for k in range(nb):
        total = total + st_buf[k, 1:2] * jnp.exp(st_buf[k, 0:1] - high)
    log_total = high + jnp.log(total)
    where = allspos[0]
    for k in range(1, n):
        where = where + allspos[k]
    ids = lax.broadcasted_iota(jnp.int32, sc.shape, 0) + b * count
    weights = (jnp.exp(sc - log_total) - (ids == where[:, :sub_all]).astype(f32)).astype(bf16)
    if feat % 128 == 0:
        doc_part = docs[:, pl.ds(pl.multiple_of(g * feat, 128), feat)]
    else:
        doc_part = docs[:, 0:feat]
        for j in range(1, ng):
            doc_part = jnp.where(g == j, docs[:, j * feat:(j + 1) * feat], doc_part)
    part = sharpness_scale * lax.dot_general(
        weights, doc_part, (((0,), (0,)), ((), ())), preferred_element_type=f32)
    for p in range(nb):
        cot_x[p] = part[p * block:(p + 1) * block].astype(bf16)
    scatter("blk", C1, cot_x, cot_buf)
    advance(2)
    mine = collect("blk", C1, cot_x, cot_buf).astype(bf16)
    cot_out[b] = mine
    spread("blk", C2, cot_out)
    mine_f = mine.astype(f32)
    for j in range(ng):
        cpiece[j] = mine_f[j * sub:(j + 1) * sub]
    for k in range(1, ng):
        p = lax.rem(g + k, ng)
        send(F3 + k, cpiece.at[p], cots_ref.at[g], (b, p))
    await_spread("blk", C2, cot_out)
    for p in range(nb):
        cot_f[p * block:(p + 1) * block] = cot_out[p].astype(f32)
    local[3].wait()
    part = lax.dot_general(cot_f[...].astype(bf16), down[...], contract_last, preferred_element_type=f32)
    for j in range(ng):
        act_x[j] = part[j * per:(j + 1) * per].astype(bf16)
    scatter("grp", A1, act_x, act_buf)
    act_out[g] = collect("grp", A1, act_x, act_buf).astype(bf16)
    spread("grp", A2, act_out)
    advance(4)
    await_spread("grp", G2, gu_out)
    await_spread("grp", A2, act_out)
    for j in range(ng):
        u_grad, g_grad = swiglu_grads(
            act_out[j].astype(f32), gu_out[j, 0:per].astype(f32), gu_out[j, per:2 * per].astype(f32))
        gg[j * per:(j + 1) * per] = g_grad
        ug[j * per:(j + 1) * per] = u_grad
    advance(2)
    part = jnp.dot(gg[...], gate[...], preferred_element_type=f32)
    part = part + jnp.dot(ug[...], up[...], preferred_element_type=f32)
    for p in range(nb):
        fin_x[p] = part[p * block:(p + 1) * block].astype(bf16)
    scatter("blk", F1, fin_x, fin_buf)
    advance(len(bulk))
    oc = 1 - core
    if direct:
        over_small(4, lambda cp: cp.wait())
    for k in range(0 if direct else np_):
        for start, gx in ((P0, g), (P1, g ^ 1), (P2, g ^ 2), (P3, g ^ 3)):
            await_recv(start + k, all_ref.at[slot(k, gx, oc)])
    own.wait()
    over_small(3, lambda cp: cp.wait())
    r, own_docs, slots = q_ref.shape[0], score_ref.shape[0], qbuf.shape[1]
    wide = slots * r
    for i in range(n):
        posrow[:, i * r:(i + 1) * r] = allpos_ref[i][:, 0:r]

    def fetch(c):
        return pltpu.make_async_copy(
            all_ref.at[pl.ds(c * slots, slots)], qbuf.at[c % 2], loc_sem.at[5 + c % 2])

    fetch(0).start()
    mine_docs = docs[pl.ds(pl.multiple_of(g * own_docs, own_docs), own_docs)]
    ids = lax.broadcasted_iota(jnp.int32, (own_docs, wide), 0) + (b * count + g * own_docs)
    t1[g] = jnp.zeros(t1.shape[1:], f32)
    for c in range(n // slots):
        if c + 1 < n // slots:
            fetch(c + 1).start()
        fetch(c).wait()
        cols = slice(c * wide, (c + 1) * wide)
        sc = sharpness_scale * lax.dot_general(
            mine_docs, qbuf[c % 2].reshape(wide, q_ref.shape[1]), contract_last, preferred_element_type=f32)
        score_ref[:, cols] = sc
        top = jnp.max(sc, axis=0, keepdims=True)
        t1[g, 0:1, cols] = top
        t1[g, 1:2, cols] = jnp.sum(jnp.exp(sc - top), axis=0, keepdims=True)
        t1[g, 2:3, cols] = jnp.sum(jnp.where(ids == posrow[:, cols], sc, 0.0), axis=0, keepdims=True)
    spread("grp", T1, t1)
    done = collect("blk", F1, fin_x, fin_buf)
    for j in range(ng):
        piece[j] = done[j * sub:(j + 1) * sub]
    for k in range(1, ng):
        p = lax.rem(g + k, ng)
        send(F2 + k, piece.at[p], grad_ref.at[g], (b, p))
    grad_ref[g] = piece[g]
    cots_ref[g] = cpiece[g]

    def merge(buf, length):
        high = buf[0, 0:1]
        for k in range(1, length):
            high = jnp.maximum(high, buf[k, 0:1])
        total, hit = jnp.zeros_like(high), jnp.zeros_like(high)
        for k in range(length):
            total = total + buf[k, 1:2] * jnp.exp(buf[k, 0:1] - high)
            hit = hit + buf[k, 2:3]
        return high, total, hit

    await_spread("grp", T1, t1)
    t2[b] = jnp.zeros(t2.shape[1:], f32)
    for i, v in enumerate(merge(t1, ng)):
        t2[b, i:i + 1] = v
    spread("blk", T2, t2)
    await_spread("blk", T2, t2)
    high, total, hit = merge(t2, nb)
    stat_ref[0:1] = high + jnp.log(total)
    stat_ref[1:2] = hit
    await_spread("grp", F2, grad_ref)
    await_spread("grp", F3, cots_ref)
    for cp in started:
        cp.wait_send()


def run_main(nb, ng, queries, pos, normed, spos, docs, gate, up, down):
    n, np_ = nb * ng, nb // 2
    sub = normed.shape[1]
    hidden, feat = gate.shape
    sub_all, block = sub * n, sub * ng
    per = sub_all // ng
    sems = 12 * np_ + 7 * ng + 5 * nb
    total = n * queries.shape[0]
    slots = max(1, 256 // queries.shape[0])
    own_docs = docs.shape[0] // ng
    V = pltpu.VMEM
    any_ = pl.BlockSpec(memory_space=pl.ANY)
    return pl.pallas_call(
        functools.partial(main_kernel, nb, ng),
        out_shape=(
            jax.ShapeDtypeStruct((n,) + queries.shape, queries.dtype),
            jax.ShapeDtypeStruct((n,) + pos.shape, pos.dtype),
            jax.ShapeDtypeStruct((ng, sub, feat), f32),
            jax.ShapeDtypeStruct((ng, sub, feat), f32),
            jax.ShapeDtypeStruct((own_docs, total), f32),
            jax.ShapeDtypeStruct((2, total), f32),
        ),
        in_specs=[VM] * 4 + [any_] * 4,
        out_specs=(any_, VM, VM, VM, VM, VM),
        scratch_shapes=[
            V((n, sub, feat), bf16), V((n, sub, queries.shape[1]), bf16), V((n,) + spos.shape, jnp.int32),
            V(docs.shape, bf16), V(gate.shape, bf16), V(up.shape, bf16), V(down.shape, bf16),
            V((sub_all, queries.shape[1]), f32), V((sub_all, feat), f32),
            V((ng, 2 * per, hidden), bf16), V((ng, 2 * per, hidden), bf16), V((ng, 2 * per, hidden), bf16),
            V((nb, 8, sub_all), f32),
            V((nb, block, feat), bf16), V((nb, block, feat), bf16), V((nb, block, feat), bf16),
            V((sub_all, feat), f32),
            V((ng, per, hidden), bf16), V((ng, per, hidden), bf16), V((ng, per, hidden), bf16),
            V((sub_all, hidden), bf16), V((sub_all, hidden), bf16),
            V((nb, block, feat), bf16), V((nb, block, feat), bf16),
            V((ng, sub, feat), f32), V((ng, sub, feat), f32),
            V((docs.shape[0], sub_all), f32),
            V((sub, queries.shape[1]), bf16),
            V((2, slots) + queries.shape, bf16), V((1, total), jnp.int32),
            V((ng, 4, total), f32), V((nb, 4, total), f32),
            DMA((7,)), DMA((sems,)), DMA((sems,)), DMA((5, n)), DMA((5, n)),
        ],
        compiler_params=params(0),
    )(queries, pos, normed, spos, docs, gate, up, down)


def row_norm(hidden):
    hidden_f = hidden.astype(f32)
    inv_rms = lax.rsqrt(jnp.mean(hidden_f * hidden_f, axis=1, keepdims=True) + epsilon)
    return (hidden_f, inv_rms)


def swiglu_grads(act_grad, gate_value, up_value):
    gate_sigmoid = jax.nn.sigmoid(gate_value)
    up_grad = (act_grad * gate_value * gate_sigmoid).astype(bf16)
    gate_grad = (
        act_grad * up_value * gate_sigmoid * (1.0 + gate_value * (1.0 - gate_sigmoid))
    ).astype(bf16)
    return (up_grad, gate_grad)


def shards(nb, ng, queries, docs, positive, last_hidden, norm_gain, gate_weight, up_weight, down_weight):
    b, g = lax.axis_index("blk"), lax.axis_index("grp")
    n, (rows, width) = nb * ng, queries.shape
    total_rows = n * rows
    sub = last_hidden.shape[0]
    sub_all = sub * n
    feat = gate_weight.shape[0]
    shard_rows = docs.shape[0]
    own_docs = shard_rows // ng

    hidden_f, inv_rms = row_norm(last_hidden)
    normed = (hidden_f * inv_rms * norm_gain).astype(bf16)
    normed = normed.reshape(sub, ng, feat).transpose(1, 0, 2)
    pos = jnp.pad(positive.reshape(1, rows), ((0, 0), (0, 128 - rows)))
    lanes = -(-sub_all // 128) * 128
    spos = lax.dynamic_update_slice(
        jnp.zeros((1, lanes), jnp.int32), positive[:sub].reshape(1, sub), (0, (b * ng + g) * sub))
    all_q, all_pos, normed_grad, cots, scores, done = run_main(
        nb, ng, queries, pos, normed, spos, docs, gate_weight.T, up_weight.T, down_weight)
    q = all_q.reshape(total_rows, width)
    pos = all_pos[:, 0, :rows].reshape(total_rows)

    ids = lax.broadcasted_iota(jnp.int32, (own_docs, 1), 0) + (b * shard_rows + g * own_docs)
    hits = ids == pos[None, :]
    log_total, pos_logit = done[0], done[1]
    losses = lax.dynamic_slice_in_dim(log_total - pos_logit, (b * ng + g) * rows, rows)
    weights = (jnp.exp(scores - log_total[None, :]) - hits.astype(f32)).astype(bf16)
    passage_grads = sharpness_scale * jnp.dot(weights, q, preferred_element_type=f32)

    normed_grad = normed_grad.transpose(1, 0, 2).reshape(sub, width)
    cots = cots.transpose(1, 0, 2).reshape(sub, width)
    scaled = normed_grad * norm_gain
    hidden_grads = (
        cots
        + inv_rms * scaled
        - hidden_f
        * inv_rms
        * inv_rms
        * inv_rms
        * jnp.mean(hidden_f * scaled, axis=1, keepdims=True)
    )
    return (losses, passage_grads, hidden_grads)


def solution(mesh):
    return jax.shard_map(
        functools.partial(shards, mesh.shape["blk"], mesh.shape["grp"]),
        mesh=mesh,
        in_specs=(
            P(("blk", "grp"), None),
            P("blk", None),
            P(("blk", "grp")),
            P(("blk", "grp"), None),
            P(),
            P("grp", "blk"),
            P("grp", "blk"),
            P("blk", "grp"),
        ),
        out_specs=(P(("blk", "grp")), P(("blk", "grp"), None), P(("blk", "grp"), None)),
        check_vma=False,
    )
```
